128 devices in a mesh: gx: 8 (over y_lo, x), gy: 16 (over y_hi, z, core).
Axes of the slice: x: 4, y: 4 (y_hi: 2, y_lo: 2; y = y_hi * 2 + y_lo), z: 4, core: 2. Of those that a mesh axis runs over, the one named last changes fastest.
Arguments:
- input_beam: float32 [2, 4096, 4096], P(None, ('gx', 'gy')), may hold values from -6 to 6
- offsets: int32 [2], replicated, may hold values from 0 to 4096
- distances: float32 [2], replicated, may hold values from 20 to 80
- screens: int32 [1, 8192, 8192], P(None, ('gx', 'gy')), may hold values from -127 to 127
- screen_scales: float32 [1, 64, 64], replicated, may hold values from 0.005 to 0.05
- last_screen: int32 [4096, 4096], P(('gx', 'gy')), may hold values from -127 to 127
- last_scales: float32 [32, 32], replicated, may hold values from 0.005 to 0.05
Outputs:
- output_beam: float32 [2, 4096, 4096], P(None, ('gx', 'gy'))
The draws below stay inside these ranges and needn't reach their ends.
All inputs are finite; a program needn't handle non-finite values.
Results may differ from the reference program's by a relative error of at most 0.0001.
Values sent between devices are 32-bit elements; how exact they have to be, the bound alone decides.
No kernel may reach another device: no remote copies, remote signals or barrier semaphores. Data moves between devices by JAX's collectives and lax.ppermute only.
A program may use at most 128 MiB of HBM per device.

```python
import math
import jax
import jax.numpy as jnp
from jax import lax

N = 8192
M = 4096
STEPS = 2


def plant(array, key, smallest, largest):
    longest = array.shape.index(max(array.shape))
    spots = []
    for shift in (0, 1):
        where = [jax.random.randint(jax.random.fold_in(key, axis), (), 0, length) for axis, length in enumerate(array.shape)]
        where[longest] = (where[longest] + shift) % array.shape[longest]
        spots.append(tuple(where))
    return array.at[spots[0]].set(smallest).at[spots[1]].set(largest)


def levels(rng, shape, cuts, low, top_value):
    level, own = 1.0, jax.random.fold_in(rng, 6)
    for position, shards_of in cuts:
        heights = jnp.exp(jax.random.uniform(jax.random.fold_in(own, position), (shards_of,), jnp.float32, low / len(cuts), top_value / len(cuts)))
        level = level * jnp.repeat(heights, shape[position] // shards_of).reshape([-1 if axis == position else 1 for axis in range(len(shape))])
    return level


def noise(rng, shape, width, limit, pieces=(), kind=jnp.bfloat16):
    drawn = width * jax.random.normal(rng, shape, jnp.float32)
    if pieces:
        drawn = drawn * levels(rng, shape, pieces, -0.22, 0.18)
    return jnp.clip(drawn, -limit, limit).astype(kind)


def setup_inputs(seed: int = 0) -> dict:
    key_of = jax.random.split(jax.random.key(seed), 8)
    input_beam = noise(key_of[0], (2, M, M), 1.0, 6.0, ((1, 128),), jnp.float32)
    offsets = jax.random.randint(key_of[1], (2,), 0, N - M + 1).astype(jnp.int32)
    distances = jnp.clip(jnp.exp(jax.random.uniform(key_of[2], (STEPS,), jnp.float32, math.log(20.0), math.log(80.0))), 20.0, 80.0)
    screens = plant(jax.random.randint(key_of[3], (STEPS - 1, N, N), -127, 128), jax.random.fold_in(key_of[3], 1), -127, 127).astype(jnp.int32)
    screen_scales = jnp.clip(jnp.exp(jax.random.uniform(key_of[4], (STEPS - 1, N // 128, N // 128), jnp.float32, math.log(0.005), math.log(0.05))), 0.005, 0.05)
    last_screen = plant(jax.random.randint(key_of[5], (M, M), -127, 128), jax.random.fold_in(key_of[5], 1), -127, 127).astype(jnp.int32)
    last_scales = jnp.clip(jnp.exp(jax.random.uniform(key_of[6], (M // 128, M // 128), jnp.float32, math.log(0.005), math.log(0.05))), 0.005, 0.05)
    return {"input_beam": input_beam, "offsets": offsets, "distances": distances, "screens": screens, "screen_scales": screen_scales, "last_screen": last_screen, "last_scales": last_scales}


def signed_index(length):
    indices = jnp.arange(length, dtype=jnp.int32)
    return jnp.where(indices < length // 2, indices, indices - length)


def expand_scales(scales):
    return jnp.repeat(jnp.repeat(scales, 128, axis=0), 128, axis=1)


def reference(input_beam, offsets, distances, screens, screen_scales, last_screen, last_scales):
    zero_index = jnp.zeros((), jnp.int32)
    grid = jnp.zeros((2, N, N), jnp.float32)
    grid = lax.dynamic_update_slice(grid, input_beam, (zero_index, offsets[0].astype(jnp.int32), offsets[1].astype(jnp.int32)))
    beam_field = grid[0] + 1j * grid[1]
    frequency = signed_index(N)
    squared = frequency[:, None] * frequency[:, None] + frequency[None, :] * frequency[None, :]
    squared_float = squared.astype(jnp.float32)
    phase_coef = (2.0 * math.pi / N) ** 2
    for layer_index in range(STEPS):
        spectrum = jnp.fft.fft2(beam_field)
        phases = squared_float * (distances[layer_index] * phase_coef)
        spectrum = spectrum * jnp.exp(-1j * phases)
        beam_field = jnp.fft.ifft2(spectrum)
        if layer_index < STEPS - 1:
            screen_phase = expand_scales(screen_scales[layer_index]) * screens[layer_index].astype(jnp.float32)
            beam_field = beam_field * jnp.exp(1j * screen_phase)
    crop_start = (N - M) // 2
    window = beam_field[crop_start:crop_start + M, crop_start:crop_start + M]
    last_phase = expand_scales(last_scales) * last_screen.astype(jnp.float32)
    window = window * jnp.exp(1j * last_phase)
    return jnp.stack([jnp.real(window), jnp.imag(window)]).astype(jnp.float32)
```

```python
import math

import jax
import jax.numpy as jnp
import numpy as np
from jax import lax
from jax.experimental import pallas as pl
from jax.experimental.pallas import tpu as pltpu
from jax.sharding import PartitionSpec as P

N = 8192
LANES = 128
AXES = ("gx", "gy")
ROOT_HALF = math.sqrt(0.5)
F32 = jnp.float32
BF16 = jnp.bfloat16


def constant_tables():
    k1 = np.arange(8)[:, None] + 8 * np.arange(8)[None, :]
    angle = -2.0 * np.pi * (k1[:, :, None] * np.arange(LANES)[None, None, :]) / N
    twiddle = np.stack([np.cos(angle), np.sin(angle)]).astype(np.float32)
    lane = np.arange(LANES)
    angle = -2.0 * np.pi * ((lane[:, None] * lane[None, :]) % LANES) / LANES
    cosine, sine = np.cos(angle), np.sin(angle)
    full = np.block([[cosine, sine], [-sine, cosine]]).astype(np.float32)
    high = full.astype(jnp.bfloat16)
    low = (full - high.astype(np.float32)).astype(jnp.bfloat16)
    return twiddle, np.concatenate([high, high, low])


def c_add(x, y):
    if x is None:
        return y
    if y is None:
        return x
    return (x[0] + y[0], x[1] + y[1])


def c_sub(x, y):
    if y is None:
        return x
    if x is None:
        return (-y[0], -y[1])
    return (x[0] - y[0], x[1] - y[1])


def c_mul(x, y):
    return (x[0] * y[0] - x[1] * y[1], x[0] * y[1] + x[1] * y[0])


def c_mul_conj(x, y):
    return (x[0] * y[0] + x[1] * y[1], x[1] * y[0] - x[0] * y[1])


def turn(x, sign):
    if x is None:
        return None
    return (-x[1], x[0]) if sign > 0 else (x[1], -x[0])


def eighth(x, sign):
    if x is None:
        return None
    if sign > 0:
        return ((x[0] - x[1]) * ROOT_HALF, (x[1] + x[0]) * ROOT_HALF)
    return ((x[0] + x[1]) * ROOT_HALF, (x[1] - x[0]) * ROOT_HALF)


def radix4(x0, x1, x2, x3, sign):
    even_sum, even_diff = c_add(x0, x2), c_sub(x0, x2)
    odd_sum, odd_diff = c_add(x1, x3), turn(c_sub(x1, x3), sign)
    return [
        c_add(even_sum, odd_sum),
        c_add(even_diff, odd_diff),
        c_sub(even_sum, odd_sum),
        c_sub(even_diff, odd_diff),
    ]


def radix8(x, sign):
    even = radix4(x[0], x[2], x[4], x[6], sign)
    odd = radix4(x[1], x[3], x[5], x[7], sign)
    odd[1] = eighth(odd[1], sign)
    odd[2] = turn(odd[2], sign)
    odd[3] = turn(eighth(odd[3], sign), sign)
    return [c_add(even[i], odd[i]) for i in range(4)] + [
        c_sub(even[i], odd[i]) for i in range(4)
    ]


def unit_root(x, index, sign):
    index = index % 64
    if index == 0:
        return x
    if index == 8:
        return eighth(x, sign)
    if index == 16:
        return turn(x, sign)
    angle = 2.0 * math.pi * index / 64
    return c_mul(x, (math.cos(angle), sign * math.sin(angle)))


def sincos(angle):
    turns = jnp.floor(angle * (2.0 / math.pi) + 0.5)
    rest = angle - turns * 1.5703125
    rest = rest - turns * 4.837512969970703125e-4
    rest = rest - turns * 7.54978995489188216e-8
    square = rest * rest
    sine = rest + rest * square * (
        -1.6666654611e-1 + square * (8.3321608736e-3 - square * 1.9515295891e-4)
    )
    cosine = (
        1.0
        - 0.5 * square
        + square
        * square
        * (4.166664568298827e-2 + square * (-1.388731625493765e-3 + square * 2.443315711809948e-5))
    )
    quarter = turns.astype(jnp.int32)
    swap = (quarter & 1) == 1
    sin_part = jnp.where(swap, cosine, sine)
    cos_part = jnp.where(swap, sine, cosine)
    sin_out = jnp.where((quarter & 2) == 2, -sin_part, sin_part)
    cos_out = jnp.where(((quarter + 1) & 2) == 2, -cos_part, cos_part)
    return cos_out, sin_out


def transfer_table(table, distance, offset):
    shape = (8, LANES)
    q_ids = lax.broadcasted_iota(jnp.int32, shape, 0)
    lane_ids = lax.broadcasted_iota(jnp.int32, shape, 1)
    coef = jnp.full(shape, distance, F32) * ((2.0 * math.pi / N) ** 2)
    coef1 = coef.astype(BF16).astype(F32)
    coef2 = (coef - coef1).astype(BF16).astype(F32)
    coef3 = (coef - coef1) - coef2
    for p in range(8):
        k = p + 8 * q_ids + 64 * lane_ids
        k = jnp.where(k < N // 2, k, k - N)
        squared = k * k
        upper = (squared & ~4095).astype(F32)
        lower = (squared & 4095).astype(F32)
        top = coef1 * upper
        turns = jnp.floor(top * (0.5 / math.pi) + 0.5)
        rest = (top - turns * 6.28125) - turns * 1.9350051879882812e-3
        rest = rest - turns * 3.0199159819567529e-7
        rest = rest + (coef2 * upper + (coef1 * lower + (coef3 * upper + coef2 * lower)))
        ramp = (k * offset) & (N - 1)
        ramp = jnp.where(ramp < N // 2, ramp, ramp - N).astype(F32) * (2.0 * math.pi / N)
        cosine, sine = sincos(rest + ramp)
        table[0, p] = cosine * (1.0 / N)
        table[1, p] = sine * (-1.0 / N)


def split_pair(first, second):
    both = jnp.concatenate([first, second], axis=0)
    high = both.astype(BF16)
    low = (both - high.astype(F32)).astype(BF16)
    return high, low


def store_split(lhs, row, values, lane):
    for half in range(4):
        high, low = split_pair(values[2 * half], values[2 * half + 1])
        rows = pl.ds(row + 16 * half, 16)
        lhs[rows, lane : lane + LANES] = high
        lhs[rows, 2 * LANES + lane : 3 * LANES + lane] = low


def product(lhs, weight):
    high, low = lhs[:, : 2 * LANES], lhs[:, 2 * LANES :]
    return jnp.dot(
        jnp.concatenate([high, low, high], axis=1), weight[...], preferred_element_type=F32
    )


def spectral_pass(field, table, twiddle, weight, lhs, result, batch):
    groups = batch // 8

    def per_p(p, carry):
        def row_of(values, part, q):
            return values[part, p, q : q + 1, :]

        for g in range(groups):
            rows = slice(8 * g, 8 * g + 8)
            x = radix8([(field[0, p, b, rows], field[1, p, b, rows]) for b in range(8)], -1)
            x = [c_mul(x[q], (row_of(twiddle, 0, q), row_of(twiddle, 1, q))) for q in range(8)]
            store_split(lhs, 64 * g, [v[0] for v in x], 0)
            store_split(lhs, 64 * g, [v[1] for v in x], LANES)
        result[...] = product(lhs, weight)
        for g in range(groups):
            x = []
            for q in range(8):
                rows = slice(64 * g + 8 * q, 64 * g + 8 * q + 8)
                value = (result[rows, :LANES], result[rows, LANES:])
                x.append(c_mul(value, (row_of(table, 0, q), row_of(table, 1, q))))
            store_split(lhs, 64 * g, [v[1] for v in x], 0)
            store_split(lhs, 64 * g, [v[0] for v in x], LANES)
        result[...] = product(lhs, weight)
        for g in range(groups):
            x = []
            for q in range(8):
                rows = slice(64 * g + 8 * q, 64 * g + 8 * q + 8)
                value = (result[rows, LANES:], result[rows, :LANES])
                x.append(c_mul_conj(value, (row_of(twiddle, 0, q), row_of(twiddle, 1, q))))
            x = radix8(x, 1)
            for b in range(8):
                rows = slice(8 * g, 8 * g + 8)
                field[0, p, b, rows] = x[b][0]
                field[1, p, b, rows] = x[b][1]
        return carry

    lax.fori_loop(0, 8, per_p, 0)


def enter(field, b, rows, x):
    x = radix8(x, -1)
    for p in range(8):
        value = unit_root(x[p], b * p, -1)
        field[0, p, b, rows] = value[0]
        field[1, p, b, rows] = value[1]


def leave(field, b, rows):
    x = [unit_root((field[0, p, b, rows], field[1, p, b, rows]), b * p, 1) for p in range(8)]
    return radix8(x, 1)


def low_half(shape):
    return lax.broadcasted_iota(jnp.int32, shape, len(shape) - 1) < LANES // 2


def swap_halves(even, odd, low):
    first = jnp.where(low, even, pltpu.roll(odd, LANES // 2, 1))
    second = jnp.where(low, pltpu.roll(even, LANES // 2, 1), odd)
    return first, second


def pack_screen_kernel(screen, packed):
    low = low_half((32, LANES))

    def per_tile(j, carry):
        tile = screen[0, :, pl.ds(pl.multiple_of(j * LANES, LANES), LANES)].astype(F32)
        even, odd = swap_halves(tile[:32], tile[32:], low)
        packed[2 * j] = even
        packed[2 * j + 1] = odd
        return carry

    lax.fori_loop(0, N // LANES, per_tile, 0, unroll=4)


def first_rows_kernel(offsets, distances, beam, twiddle, weight, moved, field, table, lhs, result):
    transfer_table(table, distances[0], offsets[1])
    low = low_half((8, LANES))

    def rows_of(g):
        return pl.ds(pl.multiple_of(g * 8, 8), 8)

    def first(g, carry):
        rows = rows_of(g)
        for b in range(8):
            x = []
            for a in range(8):
                n1 = 8 * a + b
                lanes = slice(n1 * LANES, (n1 + 1) * LANES)
                x.append((beam[0, rows, lanes], beam[1, rows, lanes]) if a < 4 else None)
            enter(field, b, rows, x)
        return carry

    lax.fori_loop(0, 4, first, 0)
    spectral_pass(field, table, twiddle, weight, lhs, result, 32)

    def last(g, carry):
        rows = rows_of(g)
        for b in range(8):
            x = leave(field, b, rows)
            for a in range(8):
                n1 = 8 * a + b
                even, odd = swap_halves(x[a][0], x[a][1], low)
                moved[2 * n1, rows] = even
                moved[2 * n1 + 1, rows] = odd
        return carry

    lax.fori_loop(0, 4, last, 0)


def columns_kernel(
    offsets, distances, scales, arrived, screen, twiddle, weight, moved,
    field, table, lhs, result, turned, phases,
):
    device = lax.axis_index(AXES)
    transfer_table(table, distances[0], offsets[0])
    lane = lax.broadcasted_iota(jnp.int32, (64, LANES), 1)

    def screens(s, carry):
        block = screen[pl.ds(pl.multiple_of(s * LANES, LANES), LANES), :].T
        upper, lower = block[:64], block[64:]
        upper32, lower32 = pltpu.roll(upper, 32, 1), pltpu.roll(lower, 32, 1)
        upper64, lower64 = pltpu.roll(upper, 64, 1), pltpu.roll(lower, 64, 1)
        upper96, lower96 = pltpu.roll(upper, 96, 1), pltpu.roll(lower, 96, 1)
        even = jnp.where(
            lane < 32, upper, jnp.where(lane < 64, lower32, jnp.where(lane < 96, upper32, lower64))
        )
        odd = jnp.where(
            lane < 32, upper64, jnp.where(lane < 64, lower96, jnp.where(lane < 96, upper96, lower))
        )
        phases[2 * s] = even * scales[0, 2 * s, device // 2]
        phases[2 * s + 1] = odd * scales[0, 2 * s + 1, device // 2]
        return carry

    lax.fori_loop(0, 32, screens, 0)

    def turn_in(n1, carry):
        turned[n1] = arrived[pl.ds(pl.multiple_of(n1 * LANES, LANES), LANES), :].T
        return carry

    lax.fori_loop(0, 32, turn_in, 0)

    def rows_of(g):
        start = pl.multiple_of(g * 8, 8)
        return pl.ds(start, 8), pl.ds(start + 64, 8)

    def first(g, carry):
        rows, rows_imag = rows_of(g)
        for b in range(8):
            x = [
                (turned[8 * a + b, rows], turned[8 * a + b, rows_imag]) if a < 4 else None
                for a in range(8)
            ]
            enter(field, b, rows, x)
        return carry

    lax.fori_loop(0, 8, first, 0)
    spectral_pass(field, table, twiddle, weight, lhs, result, 64)
    transfer_table(table, distances[1], jnp.int32(0))

    def middle(g, carry):
        rows, _ = rows_of(g)
        for b in range(8):
            x = leave(field, b, rows)
            x = [c_mul(x[a], sincos(phases[8 * a + b, rows])) for a in range(8)]
            enter(field, b, rows, x)
        return carry

    lax.fori_loop(0, 8, middle, 0)
    spectral_pass(field, table, twiddle, weight, lhs, result, 64)

    def last(g, carry):
        rows, rows_imag = rows_of(g)
        for b in range(8):
            x = leave(field, b, rows)
            for a in range(4):
                turned[8 * a + b, rows] = x[a + 2][0]
                turned[8 * a + b, rows_imag] = x[a + 2][1]
        return carry

    lax.fori_loop(0, 8, last, 0)

    def turn_out(n1, carry):
        moved[pl.ds(pl.multiple_of(n1 * LANES, LANES), LANES), :] = turned[n1].T
        return carry

    lax.fori_loop(0, 32, turn_out, 0)


def last_rows_kernel(
    distances, scales, arrived, screen, twiddle, weight, output, field, table, lhs, result
):
    device = lax.axis_index(AXES)
    transfer_table(table, distances[1], jnp.int32(0))
    low = low_half((8, LANES))

    def rows_of(g):
        return pl.ds(pl.multiple_of(g * 8, 8), 8)

    def first(g, carry):
        rows = rows_of(g)
        for b in range(8):
            x = []
            for a in range(8):
                n1 = 8 * a + b
                x.append(swap_halves(arrived[2 * n1, rows], arrived[2 * n1 + 1, rows], low))
            enter(field, b, rows, x)
        return carry

    lax.fori_loop(0, 4, first, 0)
    spectral_pass(field, table, twiddle, weight, lhs, result, 32)

    def last(g, carry):
        rows = rows_of(g)
        for b in range(8):
            x = leave(field, b, rows)
            for a in range(4):
                n1 = 8 * a + b
                lanes = slice(n1 * LANES, (n1 + 1) * LANES)
                phase = screen[rows, lanes].astype(F32) * scales[device // 4, n1]
                value = c_mul(x[a + 2], sincos(phase))
                output[0, rows, lanes] = value[0]
                output[1, rows, lanes] = value[1]
        return carry

    lax.fori_loop(0, 4, last, 0)


def call(kernel, kinds, shape, batch, extra, flops):
    space = {"s": pltpu.SMEM, "v": pltpu.VMEM}
    scratch = [
        pltpu.VMEM((2, 8, 8, batch, LANES), F32),
        pltpu.VMEM((2, 8, 8, LANES), F32),
        pltpu.VMEM((8 * batch, 4 * LANES), BF16),
        pltpu.VMEM((8 * batch, 2 * LANES), F32),
    ] if batch else []
    return pl.pallas_call(
        kernel,
        out_shape=jax.ShapeDtypeStruct(shape, F32),
        in_specs=[pl.BlockSpec(memory_space=space[kind]) for kind in kinds],
        out_specs=pl.BlockSpec(memory_space=pltpu.VMEM),
        scratch_shapes=scratch + extra,
        compiler_params=pltpu.CompilerParams(vmem_limit_bytes=48 << 20),
        cost_estimate=pl.CostEstimate(flops=flops, bytes_accessed=4 << 20, transcendentals=0),
    )


def exchange(blocks):
    return lax.all_to_all(blocks, AXES, split_axis=0, concat_axis=0, tiled=True)


def body(input_beam, offsets, distances, screens, screen_scales, last_screen, last_scales):
    twiddle, weight = (jnp.asarray(array) for array in constant_tables())
    blocks = (128, 32, LANES)
    packed = call(pack_screen_kernel, "v", blocks, 0, [], 1 << 20)(screens)
    screen_columns = exchange(packed).reshape((4096, LANES))
    moved = call(first_rows_kernel, "ssvvv", blocks, 32, [], 10**10)(
        offsets, distances, input_beam, twiddle, weight
    )
    arrived = exchange(moved).reshape((4096, LANES))
    extra = [pltpu.VMEM((32, LANES, LANES), F32), pltpu.VMEM((64, 64, LANES), F32)]
    moved = call(columns_kernel, "sssvvvv", (4096, LANES), 64, extra, 4 * 10**10)(
        offsets, distances, screen_scales, arrived, screen_columns, twiddle, weight
    )
    arrived = exchange(moved.reshape(blocks))
    return call(last_rows_kernel, "ssvvvv", (2, 32, 4096), 32, [], 10**10)(
        distances, last_scales, arrived, last_screen, twiddle, weight
    )


def solution(mesh):
    return jax.shard_map(
        body,
        mesh=mesh,
        in_specs=(
            P(None, AXES, None),
            P(),
            P(),
            P(None, AXES, None),
            P(),
            P(AXES, None),
            P(),
        ),
        out_specs=P(None, AXES, None),
        check_vma=False,
    )
```

```python
import math

import jax
import jax.numpy as jnp
import numpy as np
from jax import lax
from jax.experimental import pallas as pl
from jax.experimental.pallas import tpu as pltpu
from jax.sharding import PartitionSpec as P

N = 8192
LANES = 128
AXES = ("gx", "gy")
ROOT_HALF = math.sqrt(0.5)
SINE = [
    math.sqrt(2.0) * term
    for term in (3.14159264013, -5.16771008351, 2.55007752321, -0.598291285620, 0.0776576603045)
]
COSINE = [
    math.sqrt(2.0) * term
    for term in (0.999999953248, -4.93479283062, 4.05841135286, -1.33187656808, 0.219689611098)
]
F32 = jnp.float32
BF16 = jnp.bfloat16


def constant_tables():
    k1 = np.arange(8)[:, None] + 8 * np.arange(8)[None, :]
    angle = -2.0 * np.pi * (k1[:, :, None] * np.arange(LANES)[None, None, :]) / N
    twiddle = np.stack([np.cos(angle), np.sin(angle)]).astype(np.float32)
    lane = np.arange(LANES)
    angle = -2.0 * np.pi * ((lane[:, None] * lane[None, :]) % LANES) / LANES
    cosine, sine = np.cos(angle), np.sin(angle)
    full = np.block([[cosine, sine], [-sine, cosine]]).astype(np.float32)
    high = full.astype(jnp.bfloat16)
    low = (full - high.astype(np.float32)).astype(jnp.bfloat16)
    return twiddle, np.concatenate([high, high, low])


def c_add(x, y):
    if x is None:
        return y
    if y is None:
        return x
    return (x[0] + y[0], x[1] + y[1])


def c_sub(x, y):
    if y is None:
        return x
    if x is None:
        return (-y[0], -y[1])
    return (x[0] - y[0], x[1] - y[1])


def c_mul(x, y):
    return (x[0] * y[0] - x[1] * y[1], x[0] * y[1] + x[1] * y[0])


def c_mul_conj(x, y):
    return (x[0] * y[0] + x[1] * y[1], x[1] * y[0] - x[0] * y[1])


def turn(x, sign):
    if x is None:
        return None
    return (-x[1], x[0]) if sign > 0 else (x[1], -x[0])


def eighth(x, sign):
    if x is None:
        return None
    if sign > 0:
        return ((x[0] - x[1]) * ROOT_HALF, (x[1] + x[0]) * ROOT_HALF)
    return ((x[0] + x[1]) * ROOT_HALF, (x[1] - x[0]) * ROOT_HALF)


def radix4(x0, x1, x2, x3, sign):
    even_sum, even_diff = c_add(x0, x2), c_sub(x0, x2)
    odd_sum, odd_diff = c_add(x1, x3), turn(c_sub(x1, x3), sign)
    return [
        c_add(even_sum, odd_sum),
        c_add(even_diff, odd_diff),
        c_sub(even_sum, odd_sum),
        c_sub(even_diff, odd_diff),
    ]


def radix8(x, sign):
    even = radix4(x[0], x[2], x[4], x[6], sign)
    odd = radix4(x[1], x[3], x[5], x[7], sign)
    odd[1] = eighth(odd[1], sign)
    odd[2] = turn(odd[2], sign)
    odd[3] = turn(eighth(odd[3], sign), sign)
    return [c_add(even[i], odd[i]) for i in range(4)] + [
        c_sub(even[i], odd[i]) for i in range(4)
    ]


def unit_root(x, index, sign):
    index = index % 64
    if index == 0:
        return x
    if index == 8:
        return eighth(x, sign)
    if index == 16:
        return turn(x, sign)
    angle = 2.0 * math.pi * index / 64
    return c_mul(x, (math.cos(angle), sign * math.sin(angle)))


def sincos(angle):
    turns = jnp.floor(angle * (2.0 / math.pi) + 0.5)
    rest = angle - turns * 1.5703125
    rest = rest - turns * 4.837512969970703125e-4
    rest = rest - turns * 7.54978995489188216e-8
    square = rest * rest
    sine = rest + rest * square * (
        -1.6666654611e-1 + square * (8.3321608736e-3 - square * 1.9515295891e-4)
    )
    cosine = (
        1.0
        - 0.5 * square
        + square
        * square
        * (4.166664568298827e-2 + square * (-1.388731625493765e-3 + square * 2.443315711809948e-5))
    )
    quarter = turns.astype(jnp.int32)
    swap = (quarter & 1) == 1
    sin_part = jnp.where(swap, cosine, sine)
    cos_part = jnp.where(swap, sine, cosine)
    sin_out = jnp.where((quarter & 2) == 2, -sin_part, sin_part)
    cos_out = jnp.where(((quarter + 1) & 2) == 2, -cos_part, cos_part)
    return cos_out, sin_out


def phasor(turns):
    rest = turns - jnp.floor(turns + 0.5)
    square = rest * rest
    sine = rest * (
        SINE[0]
        + square * (SINE[1] + square * (SINE[2] + square * (SINE[3] + square * SINE[4])))
    )
    cosine = COSINE[0] + square * (
        COSINE[1] + square * (COSINE[2] + square * (COSINE[3] + square * COSINE[4]))
    )
    return 1.0 - sine * sine, sine * cosine


def transfer_table(table, distance, offset):
    shape = (8, LANES)
    q_ids = lax.broadcasted_iota(jnp.int32, shape, 0)
    lane_ids = lax.broadcasted_iota(jnp.int32, shape, 1)
    coef = jnp.full(shape, distance, F32) * ((2.0 * math.pi / N) ** 2)
    coef1 = coef.astype(BF16).astype(F32)
    coef2 = (coef - coef1).astype(BF16).astype(F32)
    coef3 = (coef - coef1) - coef2
    for p in range(8):
        k = p + 8 * q_ids + 64 * lane_ids
        k = jnp.where(k < N // 2, k, k - N)
        squared = k * k
        upper = (squared & ~4095).astype(F32)
        lower = (squared & 4095).astype(F32)
        top = coef1 * upper
        turns = jnp.floor(top * (0.5 / math.pi) + 0.5)
        rest = (top - turns * 6.28125) - turns * 1.9350051879882812e-3
        rest = rest - turns * 3.0199159819567529e-7
        rest = rest + (coef2 * upper + (coef1 * lower + (coef3 * upper + coef2 * lower)))
        ramp = (k * offset) & (N - 1)
        ramp = jnp.where(ramp < N // 2, ramp, ramp - N).astype(F32) * (2.0 * math.pi / N)
        cosine, sine = sincos(rest + ramp)
        table[0, p] = cosine * (1.0 / N)
        table[1, p] = sine * (-1.0 / N)


def split_pair(first, second):
    both = jnp.concatenate([first, second], axis=0)
    high = both.astype(BF16)
    low = (both - high.astype(F32)).astype(BF16)
    return high, low


def store_split(lhs, row, values, lane):
    for half in range(4):
        high, low = split_pair(values[2 * half], values[2 * half + 1])
        rows = pl.ds(row + 16 * half, 16)
        lhs[rows, lane : lane + LANES] = high
        lhs[rows, 2 * LANES + lane : 3 * LANES + lane] = low


def product(lhs, weight):
    high, low = lhs[:, : 2 * LANES], lhs[:, 2 * LANES :]
    return jnp.dot(
        jnp.concatenate([high, low, high], axis=1), weight[...], preferred_element_type=F32
    )


def spectral_pass(field, table, twiddle, weight, left, result, batch):
    groups = batch // 8
    width = 64 // batch
    steps = 8 // width

    def row_of(values, part, p, q):
        return values[part, p, q : q + 1, :]

    def places(step):
        for j in range(width):
            for g in range(groups):
                yield step * width + j, slice(8 * g, 8 * g + 8), 64 * (groups * j + g)

    def result_rows(row, q):
        return slice(row + 8 * q, row + 8 * q + 8)

    def forward(step, lhs):
        for p, rows, row in places(step):
            x = radix8([(field[0, p, b, rows], field[1, p, b, rows]) for b in range(8)], -1)
            x = [
                c_mul(x[q], (row_of(twiddle, 0, p, q), row_of(twiddle, 1, p, q)))
                for q in range(8)
            ]
            store_split(lhs, row, [v[0] for v in x], 0)
            store_split(lhs, row, [v[1] for v in x], LANES)

    def transfer(step, values, lhs):
        for p, rows, row in places(step):
            x = []
            for q in range(8):
                at = result_rows(row, q)
                value = (values[at, :LANES], values[at, LANES:])
                x.append(c_mul(value, (row_of(table, 0, p, q), row_of(table, 1, p, q))))
            store_split(lhs, row, [v[1] for v in x], 0)
            store_split(lhs, row, [v[0] for v in x], LANES)

    def inverse(step, values):
        for p, rows, row in places(step):
            x = []
            for q in range(8):
                at = result_rows(row, q)
                value = (values[at, LANES:], values[at, :LANES])
                x.append(
                    c_mul_conj(value, (row_of(twiddle, 0, p, q), row_of(twiddle, 1, p, q)))
                )
            x = radix8(x, 1)
            for b in range(8):
                field[0, p, b, rows] = x[b][0]
                field[1, p, b, rows] = x[b][1]

    def multiply(lhs, values):
        values[...] = product(lhs, weight)

    forward_left, inverse_left = left[:2], left[2:]
    forward_result, inverse_result = result[:2], result[2:]
    forward(0, forward_left[0])
    multiply(forward_left[0], forward_result[0])
    forward(1, forward_left[1])
    multiply(forward_left[1], forward_result[1])
    transfer(0, forward_result[0], inverse_left[0])
    multiply(inverse_left[0], inverse_result[0])
    forward(2, forward_left[0])

    def two_steps(i, carry):
        step = 2 * i
        multiply(forward_left[0], forward_result[0])
        transfer(step - 1, forward_result[1], inverse_left[1])
        multiply(inverse_left[1], inverse_result[1])
        inverse(step - 2, inverse_result[0])
        forward(step + 1, forward_left[1])
        multiply(forward_left[1], forward_result[1])
        transfer(step, forward_result[0], inverse_left[0])
        multiply(inverse_left[0], inverse_result[0])
        inverse(step - 1, inverse_result[1])
        forward(jnp.minimum(step + 2, steps - 1), forward_left[0])
        return carry

    lax.fori_loop(1, steps // 2, two_steps, 0)
    transfer(steps - 1, forward_result[1], inverse_left[1])
    multiply(inverse_left[1], inverse_result[1])
    inverse(steps - 2, inverse_result[0])
    inverse(steps - 1, inverse_result[1])


def enter(field, b, rows, x):
    x = radix8(x, -1)
    for p in range(8):
        value = unit_root(x[p], b * p, -1)
        field[0, p, b, rows] = value[0]
        field[1, p, b, rows] = value[1]


def leave(field, b, rows):
    x = [unit_root((field[0, p, b, rows], field[1, p, b, rows]), b * p, 1) for p in range(8)]
    return radix8(x, 1)


def low_half(shape):
    return lax.broadcasted_iota(jnp.int32, shape, len(shape) - 1) < LANES // 2


def swap_halves(even, odd, low):
    first = jnp.where(low, even, pltpu.roll(odd, LANES // 2, 1))
    second = jnp.where(low, pltpu.roll(even, LANES // 2, 1), odd)
    return first, second


def eight_rows(g):
    return pl.ds(pl.multiple_of(g * 8, 8), 8)


def pack_screen(scales, screen, moved, device):
    low = low_half((32, LANES))

    def per_pair(j, carry):
        tiles = []
        for half in range(2):
            lanes = pl.ds(pl.multiple_of(j * (2 * LANES), 2 * LANES) + half * LANES, LANES)
            scale = scales[0, device // 2, 2 * j + half] * (0.5 / math.pi)
            tiles.append(screen[0, :, lanes].astype(F32) * scale)
        block = jnp.concatenate(tiles, axis=0).T
        for half in range(2):
            part = block[64 * half : 64 * half + 64]
            first, second = swap_halves(part[:32], part[32:], low)
            moved[4 * j + half, 32:] = first
            moved[4 * j + 2 + half, 32:] = second
        return carry

    lax.fori_loop(0, N // (2 * LANES), per_pair, 0, unroll=2)


def first_rows_kernel(
    offsets_in, distances_in, scales_in, beam_in, screen_in, twiddle_in, weight_in, moved,
    field, table, l0, l1, l2, l3, r0, r1, r2, r3,
    offsets, distances, scales, beam, screen, twiddle, weight, blocks, arrival, departure,
):
    pairs = (
        (offsets_in, offsets), (distances_in, distances), (scales_in, scales),
        (screen_in, screen), (beam_in, beam), (twiddle_in, twiddle), (weight_in, weight),
    )
    copies = [
        pltpu.make_async_copy(source, target, arrival.at[i])
        for i, (source, target) in enumerate(pairs)
    ]
    for copy in copies:
        copy.start()
    device = lax.axis_index(AXES)
    for copy in copies[:2]:
        copy.wait()
    transfer_table(table, distances[0], offsets[1])
    for copy in copies[2:4]:
        copy.wait()
    pack_screen(scales, screen, blocks, device)

    def leaving(part):
        rows = slice(32, 64) if part == 4 else slice(8 * part, 8 * part + 8)
        return pltpu.make_async_copy(blocks.at[:, rows], moved.at[:, rows], departure.at[part])

    leaving(4).start()
    for copy in copies[4:]:
        copy.wait()
    low = low_half((8, LANES))

    def first(g, carry):
        rows = eight_rows(g)
        for b in range(8):
            x = []
            for a in range(8):
                n1 = 8 * a + b
                lanes = slice(n1 * LANES, (n1 + 1) * LANES)
                x.append((beam[0, rows, lanes], beam[1, rows, lanes]) if a < 4 else None)
            enter(field, b, rows, x)
        return carry

    lax.fori_loop(0, 4, first, 0)
    spectral_pass(field, table, twiddle, weight, (l0, l1, l2, l3), (r0, r1, r2, r3), 32)

    def last(g):
        rows = slice(8 * g, 8 * g + 8)
        for b in range(8):
            x = leave(field, b, rows)
            for a in range(8):
                n1 = 8 * a + b
                even, odd = swap_halves(x[a][0], x[a][1], low)
                blocks[2 * n1, rows] = even
                blocks[2 * n1 + 1, rows] = odd
        leaving(g).start()

    for g in range(4):
        last(g)
    for part in range(5):
        leaving(part).wait()


def columns_kernel(
    offsets, distances, arrived, twiddle, weight, moved,
    field, table, l0, l1, l2, l3, r0, r1, r2, r3, turned,
):
    transfer_table(table, distances[0], offsets[0])

    def turn_in(n1, carry):
        turned[n1] = arrived[pl.ds(4 * n1, 4), :32].reshape((LANES, LANES)).T
        return carry

    lax.fori_loop(0, 32, turn_in, 0, unroll=4)

    def first(g, carry):
        rows, rows_imag = eight_rows(g), eight_rows(g + 8)
        for b in range(8):
            x = [
                (turned[8 * a + b, rows], turned[8 * a + b, rows_imag]) if a < 4 else None
                for a in range(8)
            ]
            enter(field, b, rows, x)
        return carry

    lax.fori_loop(0, 8, first, 0)
    spectral_pass(field, table, twiddle, weight, (l0, l1, l2, l3), (r0, r1, r2, r3), 64)
    transfer_table(table, distances[1], jnp.int32(0))
    low = low_half((8, LANES))

    def middle(g, carry):
        for half in range(2):
            rows = eight_rows(g + 4 * half)
            for b in range(8):
                x = leave(field, b, rows)
                for a in range(8):
                    n1 = 8 * a + b
                    even, odd = arrived[2 * n1, eight_rows(g + 4)], arrived[2 * n1 + 1, eight_rows(g + 4)]
                    turns = swap_halves(even, odd, low)[half]
                    x[a] = c_mul(x[a], phasor(turns))
                enter(field, b, rows, x)
        return carry

    lax.fori_loop(0, 4, middle, 0)
    spectral_pass(field, table, twiddle, weight, (l0, l1, l2, l3), (r0, r1, r2, r3), 64)

    def last(g, carry):
        rows, rows_imag = eight_rows(g), eight_rows(g + 8)
        for b in range(8):
            x = leave(field, b, rows)
            for a in range(4):
                turned[8 * a + b, rows] = x[a + 2][0]
                turned[8 * a + b, rows_imag] = x[a + 2][1]
        return carry

    lax.fori_loop(0, 8, last, 0)

    def turn_out(n1, carry):
        moved[pl.ds(pl.multiple_of(n1 * LANES, LANES), LANES), :] = turned[n1].T
        return carry

    lax.fori_loop(0, 32, turn_out, 0, unroll=4)


def last_rows_kernel(
    distances, scales, arrived, screen, twiddle, weight, output,
    field, table, l0, l1, l2, l3, r0, r1, r2, r3,
):
    device = lax.axis_index(AXES)
    transfer_table(table, distances[1], jnp.int32(0))
    low = low_half((8, LANES))

    def first(g, carry):
        rows = eight_rows(g)
        for b in range(8):
            x = []
            for a in range(8):
                n1 = 8 * a + b
                x.append(swap_halves(arrived[2 * n1, rows], arrived[2 * n1 + 1, rows], low))
            enter(field, b, rows, x)
        return carry

    lax.fori_loop(0, 4, first, 0)
    spectral_pass(field, table, twiddle, weight, (l0, l1, l2, l3), (r0, r1, r2, r3), 32)

    def last(g, carry):
        rows = eight_rows(g)
        for b in range(8):
            x = leave(field, b, rows)
            for a in range(4):
                n1 = 8 * a + b
                lanes = slice(n1 * LANES, (n1 + 1) * LANES)
                scale = scales[device // 4, n1] * (0.5 / math.pi)
                value = c_mul(x[a + 2], phasor(screen[rows, lanes].astype(F32) * scale))
                output[0, rows, lanes] = value[0]
                output[1, rows, lanes] = value[1]
        return carry

    lax.fori_loop(0, 4, last, 0)


def call(kernel, kinds, shape, batch, extra, flops, out_kind="v", limit=40):
    space = {"s": pltpu.SMEM, "v": pltpu.VMEM, "h": pltpu.HBM}
    scratch = [
        pltpu.VMEM((2, 8, 8, batch, LANES), F32),
        pltpu.VMEM((2, 8, 8, LANES), F32),
        *[pltpu.VMEM((512, 4 * LANES), BF16)] * 4,
        *[pltpu.VMEM((512, 2 * LANES), F32)] * 4,
    ]
    return pl.pallas_call(
        kernel,
        out_shape=jax.ShapeDtypeStruct(shape, F32),
        in_specs=[pl.BlockSpec(memory_space=space[kind]) for kind in kinds],
        out_specs=pl.BlockSpec(memory_space=space[out_kind]),
        scratch_shapes=scratch + extra,
        compiler_params=pltpu.CompilerParams(vmem_limit_bytes=limit << 20),
        cost_estimate=pl.CostEstimate(flops=flops, bytes_accessed=4 << 20, transcendentals=0),
    )


def exchange(blocks):
    return lax.all_to_all(blocks, AXES, split_axis=0, concat_axis=0, tiled=True)


def body(input_beam, offsets, distances, screens, screen_scales, last_screen, last_scales):
    twiddle, weight = (jnp.asarray(array) for array in constant_tables())
    extra = [
        pltpu.SMEM((2,), jnp.int32),
        pltpu.SMEM((2,), F32),
        pltpu.SMEM((1, 64, 64), F32),
        pltpu.VMEM((2, 32, 4096), F32),
        pltpu.VMEM((1, 64, N), jnp.int32),
        pltpu.VMEM(twiddle.shape, F32),
        pltpu.VMEM(weight.shape, BF16),
        pltpu.VMEM((128, 64, LANES), F32),
        pltpu.SemaphoreType.DMA((7,)),
        pltpu.SemaphoreType.DMA((5,)),
    ]
    moved = call(
        first_rows_kernel, "hhhhhhh", (128, 64, LANES), 32, extra, 10**10, "h", 60
    )(
        offsets, distances, screen_scales, input_beam, screens, twiddle, weight
    )
    extra = [pltpu.VMEM((32, LANES, LANES), F32)]
    moved = call(columns_kernel, "ssvvv", (4096, LANES), 64, extra, 4 * 10**10)(
        offsets, distances, exchange(moved), twiddle, weight
    )
    arrived = exchange(moved.reshape((128, 32, LANES)))
    return call(last_rows_kernel, "ssvvvv", (2, 32, 4096), 32, [], 10**10)(
        distances, last_scales, arrived, last_screen, twiddle, weight
    )


def solution(mesh):
    return jax.shard_map(
        body,
        mesh=mesh,
        in_specs=(
            P(None, AXES, None),
            P(),
            P(),
            P(None, AXES, None),
            P(),
            P(AXES, None),
            P(),
        ),
        out_specs=P(None, AXES, None),
        check_vma=False,
    )
```

```python
import math

import jax
import jax.numpy as jnp
import numpy as np
from jax import lax
from jax.experimental import pallas as pl
from jax.experimental.pallas import tpu as pltpu
from jax.sharding import PartitionSpec as P

N = 8192
LANES = 128
AXES = ("gx", "gy")
ROOT_HALF = math.sqrt(0.5)
SINE = [
    math.sqrt(2.0) * term
    for term in (3.14159264013, -5.16771008351, 2.55007752321, -0.598291285620, 0.0776576603045)
]
COSINE = [
    math.sqrt(2.0) * term
    for term in (0.999999953248, -4.93479283062, 4.05841135286, -1.33187656808, 0.219689611098)
]
F32 = jnp.float32
BF16 = jnp.bfloat16


def constant_tables():
    k1 = np.arange(8)[:, None] + 8 * np.arange(8)[None, :]
    angle = -2.0 * np.pi * (k1[:, :, None] * np.arange(LANES)[None, None, :]) / N
    twiddle = np.stack([np.cos(angle), np.sin(angle)]).astype(np.float32)
    lane = np.arange(LANES)
    angle = -2.0 * np.pi * ((lane[:, None] * lane[None, :]) % LANES) / LANES
    cosine, sine = np.cos(angle), np.sin(angle)
    full = np.block([[cosine, sine], [-sine, cosine]]).astype(np.float32)
    high = full.astype(jnp.bfloat16)
    low = (full - high.astype(np.float32)).astype(jnp.bfloat16)
    return twiddle, np.concatenate([high, high, low])


def c_add(x, y):
    if x is None:
        return y
    if y is None:
        return x
    return (x[0] + y[0], x[1] + y[1])


def c_sub(x, y):
    if y is None:
        return x
    if x is None:
        return (-y[0], -y[1])
    return (x[0] - y[0], x[1] - y[1])


def c_mul(x, y):
    return (x[0] * y[0] - x[1] * y[1], x[0] * y[1] + x[1] * y[0])


def c_mul_conj(x, y):
    return (x[0] * y[0] + x[1] * y[1], x[1] * y[0] - x[0] * y[1])


def turn(x, sign):
    if x is None:
        return None
    return (-x[1], x[0]) if sign > 0 else (x[1], -x[0])


def eighth(x, sign):
    if x is None:
        return None
    if sign > 0:
        return ((x[0] - x[1]) * ROOT_HALF, (x[1] + x[0]) * ROOT_HALF)
    return ((x[0] + x[1]) * ROOT_HALF, (x[1] - x[0]) * ROOT_HALF)


def radix4(x0, x1, x2, x3, sign):
    even_sum, even_diff = c_add(x0, x2), c_sub(x0, x2)
    odd_sum, odd_diff = c_add(x1, x3), turn(c_sub(x1, x3), sign)
    return [
        c_add(even_sum, odd_sum),
        c_add(even_diff, odd_diff),
        c_sub(even_sum, odd_sum),
        c_sub(even_diff, odd_diff),
    ]


def radix8(x, sign):
    even = radix4(x[0], x[2], x[4], x[6], sign)
    odd = radix4(x[1], x[3], x[5], x[7], sign)
    odd[1] = eighth(odd[1], sign)
    odd[2] = turn(odd[2], sign)
    odd[3] = turn(eighth(odd[3], sign), sign)
    return [c_add(even[i], odd[i]) for i in range(4)] + [
        c_sub(even[i], odd[i]) for i in range(4)
    ]


def unit_root(x, index, sign):
    index = index % 64
    if index == 0:
        return x
    if index == 8:
        return eighth(x, sign)
    if index == 16:
        return turn(x, sign)
    angle = 2.0 * math.pi * index / 64
    return c_mul(x, (math.cos(angle), sign * math.sin(angle)))


def sincos(angle):
    turns = jnp.floor(angle * (2.0 / math.pi) + 0.5)
    rest = angle - turns * 1.5703125
    rest = rest - turns * 4.837512969970703125e-4
    rest = rest - turns * 7.54978995489188216e-8
    square = rest * rest
    sine = rest + rest * square * (
        -1.6666654611e-1 + square * (8.3321608736e-3 - square * 1.9515295891e-4)
    )
    cosine = (
        1.0
        - 0.5 * square
        + square
        * square
        * (4.166664568298827e-2 + square * (-1.388731625493765e-3 + square * 2.443315711809948e-5))
    )
    quarter = turns.astype(jnp.int32)
    swap = (quarter & 1) == 1
    sin_part = jnp.where(swap, cosine, sine)
    cos_part = jnp.where(swap, sine, cosine)
    sin_out = jnp.where((quarter & 2) == 2, -sin_part, sin_part)
    cos_out = jnp.where(((quarter + 1) & 2) == 2, -cos_part, cos_part)
    return cos_out, sin_out


def phasor(turns):
    rest = turns - jnp.floor(turns + 0.5)
    square = rest * rest
    sine = rest * (
        SINE[0]
        + square * (SINE[1] + square * (SINE[2] + square * (SINE[3] + square * SINE[4])))
    )
    cosine = COSINE[0] + square * (
        COSINE[1] + square * (COSINE[2] + square * (COSINE[3] + square * COSINE[4]))
    )
    return 1.0 - sine * sine, sine * cosine


def transfer_table(table, at, distance, offset):
    shape = (8, LANES)
    q_ids = lax.broadcasted_iota(jnp.int32, shape, 0)
    lane_ids = lax.broadcasted_iota(jnp.int32, shape, 1)
    coef = jnp.full(shape, distance, F32) * ((2.0 * math.pi / N) ** 2)
    coef1 = coef.astype(BF16).astype(F32)
    coef2 = (coef - coef1).astype(BF16).astype(F32)
    coef3 = (coef - coef1) - coef2
    for p in range(8):
        k = p + 8 * q_ids + 64 * lane_ids
        k = jnp.where(k < N // 2, k, k - N)
        squared = k * k
        upper = (squared & ~4095).astype(F32)
        lower = (squared & 4095).astype(F32)
        top = coef1 * upper
        turns = jnp.floor(top * (0.5 / math.pi) + 0.5)
        rest = (top - turns * 6.28125) - turns * 1.9350051879882812e-3
        rest = rest - turns * 3.0199159819567529e-7
        rest = rest + (coef2 * upper + (coef1 * lower + (coef3 * upper + coef2 * lower)))
        ramp = (k * offset) & (N - 1)
        ramp = jnp.where(ramp < N // 2, ramp, ramp - N).astype(F32) * (2.0 * math.pi / N)
        cosine, sine = sincos(rest + ramp)
        table[at, 0, p] = cosine * (1.0 / N)
        table[at, 1, p] = sine * (-1.0 / N)


def split_pair(first, second):
    both = jnp.concatenate([first, second], axis=0)
    high = both.astype(BF16)
    low = (both - high.astype(F32)).astype(BF16)
    return high, low


def store_split(lhs, row, values, lane):
    for half in range(4):
        high, low = split_pair(values[2 * half], values[2 * half + 1])
        rows = pl.ds(row + 16 * half, 16)
        lhs[rows, lane : lane + LANES] = high
        lhs[rows, 2 * LANES + lane : 3 * LANES + lane] = low


def product(lhs, weight):
    high, low = lhs[:, : 2 * LANES], lhs[:, 2 * LANES :]
    return jnp.dot(
        jnp.concatenate([high, low, high], axis=1), weight[...], preferred_element_type=F32
    )


def spectral_pass(field, table, twiddle, weight, left, result, batch, side=None):
    groups = batch // 8
    width = 64 // batch
    steps = 8 // width

    def row_of(values, part, p, q):
        return values[part, p, q : q + 1, :]

    def table_row(part, p, q):
        values, at = table
        return values[at, part, p, q : q + 1, :]

    def places(step):
        for j in range(width):
            for g in range(groups):
                yield step * width + j, slice(8 * g, 8 * g + 8), 64 * (groups * j + g)

    def result_rows(row, q):
        return slice(row + 8 * q, row + 8 * q + 8)

    def forward(step, lhs):
        for i, (p, rows, row) in enumerate(places(step)):
            if side is not None:
                side(step, i)
            x = radix8([(field[0, p, b, rows], field[1, p, b, rows]) for b in range(8)], -1)
            x = [
                c_mul(x[q], (row_of(twiddle, 0, p, q), row_of(twiddle, 1, p, q)))
                for q in range(8)
            ]
            store_split(lhs, row, [v[0] for v in x], 0)
            store_split(lhs, row, [v[1] for v in x], LANES)

    def transfer(step, values, lhs):
        for p, rows, row in places(step):
            x = []
            for q in range(8):
                at = result_rows(row, q)
                value = (values[at, :LANES], values[at, LANES:])
                x.append(c_mul(value, (table_row(0, p, q), table_row(1, p, q))))
            store_split(lhs, row, [v[1] for v in x], 0)
            store_split(lhs, row, [v[0] for v in x], LANES)

    def inverse(step, values):
        for p, rows, row in places(step):
            x = []
            for q in range(8):
                at = result_rows(row, q)
                value = (values[at, LANES:], values[at, :LANES])
                x.append(
                    c_mul_conj(value, (row_of(twiddle, 0, p, q), row_of(twiddle, 1, p, q)))
                )
            x = radix8(x, 1)
            for b in range(8):
                field[0, p, b, rows] = x[b][0]
                field[1, p, b, rows] = x[b][1]

    def multiply(lhs, values):
        values[...] = product(lhs, weight)

    forward_left, inverse_left = left[:2], left[2:]
    forward_result, inverse_result = result[:2], result[2:]
    forward(0, forward_left[0])
    multiply(forward_left[0], forward_result[0])
    forward(1, forward_left[1])
    multiply(forward_left[1], forward_result[1])
    transfer(0, forward_result[0], inverse_left[0])
    multiply(inverse_left[0], inverse_result[0])
    forward(2, forward_left[0])

    def two_steps(i, carry, more=True):
        step = 2 * i
        multiply(forward_left[0], forward_result[0])
        transfer(step - 1, forward_result[1], inverse_left[1])
        multiply(inverse_left[1], inverse_result[1])
        inverse(step - 2, inverse_result[0])
        forward(step + 1, forward_left[1])
        multiply(forward_left[1], forward_result[1])
        transfer(step, forward_result[0], inverse_left[0])
        multiply(inverse_left[0], inverse_result[0])
        inverse(step - 1, inverse_result[1])
        if more:
            forward(step + 2, forward_left[0])
        return carry

    if steps > 4:
        lax.fori_loop(1, steps // 2 - 1, two_steps, 0)
    two_steps(steps // 2 - 1, 0, more=False)
    transfer(steps - 1, forward_result[1], inverse_left[1])
    multiply(inverse_left[1], inverse_result[1])
    inverse(steps - 2, inverse_result[0])
    inverse(steps - 1, inverse_result[1])


def enter(field, b, rows, x):
    x = radix8(x, -1)
    for p in range(8):
        value = unit_root(x[p], b * p, -1)
        field[0, p, b, rows] = value[0]
        field[1, p, b, rows] = value[1]


def leave(field, b, rows):
    x = [unit_root((field[0, p, b, rows], field[1, p, b, rows]), b * p, 1) for p in range(8)]
    return radix8(x, 1)


def low_half(shape):
    return lax.broadcasted_iota(jnp.int32, shape, len(shape) - 1) < LANES // 2


def swap_halves(even, odd, low):
    first = jnp.where(low, even, pltpu.roll(odd, LANES // 2, 1))
    second = jnp.where(low, pltpu.roll(even, LANES // 2, 1), odd)
    return first, second


def eight_rows(g):
    return pl.ds(g * 8 if isinstance(g, int) else pl.multiple_of(g * 8, 8), 8)


def pack_screen(j, scales, screen, moved, device, low):
    tiles = []
    for half in range(2):
        start = j * (2 * LANES) + half * LANES
        lanes = pl.ds(start if isinstance(j, int) else pl.multiple_of(start, LANES), LANES)
        scale = scales[0, device // 2, 2 * j + half] * (0.5 / math.pi)
        tiles.append(screen[0, :, lanes].astype(F32) * scale)
    block = jnp.concatenate(tiles, axis=0).T
    for half in range(2):
        part = block[64 * half : 64 * half + 64]
        first, second = swap_halves(part[:32], part[32:], low)
        moved[4 * j + half, 32:] = first
        moved[4 * j + 2 + half, 32:] = second


def first_rows_kernel(
    offsets_in, distances_in, scales_in, beam_in, screen_in, twiddle_in, weight_in, moved,
    field, l0, l1, l2, l3, r0, r1, r2, r3, table,
    offsets, distances, scales, beam, screen, twiddle, weight, blocks, arrival, departure,
):
    pairs = (
        (offsets_in, offsets), (distances_in, distances), (scales_in, scales),
        (beam_in, beam), (twiddle_in, twiddle), (weight_in, weight), (screen_in, screen),
    )
    copies = [
        pltpu.make_async_copy(source, target, arrival.at[i])
        for i, (source, target) in enumerate(pairs)
    ]
    for copy in copies:
        copy.start()
    device = lax.axis_index(AXES)
    for copy in copies[:2]:
        copy.wait()
    transfer_table(table, 0, distances[0], offsets[1])
    copies[3].wait()

    def leaving(part):
        rows = slice(32, 64) if part == 4 else slice(8 * part, 8 * part + 8)
        return pltpu.make_async_copy(blocks.at[:, rows], moved.at[:, rows], departure.at[part])

    low = low_half((8, LANES))

    def first(g, carry):
        rows = eight_rows(g)
        for b in range(8):
            x = []
            for a in range(8):
                n1 = 8 * a + b
                lanes = slice(n1 * LANES, (n1 + 1) * LANES)
                x.append((beam[0, rows, lanes], beam[1, rows, lanes]) if a < 4 else None)
            enter(field, b, rows, x)
        return carry

    lax.fori_loop(0, 4, first, 0)
    for copy in (copies[2], *copies[4:]):
        copy.wait()
    low_packed = low_half((32, LANES))
    spectral_pass(
        field, (table, 0), twiddle, weight, (l0, l1, l2, l3), (r0, r1, r2, r3), 32,
        lambda step, i: pack_screen(8 * step + i, scales, screen, blocks, device, low_packed),
    )
    leaving(4).start()

    def last(g):
        rows = slice(8 * g, 8 * g + 8)
        for b in range(8):
            x = leave(field, b, rows)
            for a in range(8):
                n1 = 8 * a + b
                even, odd = swap_halves(x[a][0], x[a][1], low)
                blocks[2 * n1, rows] = even
                blocks[2 * n1 + 1, rows] = odd
        leaving(g).start()

    for g in range(4):
        last(g)
    for part in range(5):
        leaving(part).wait()


def tables_kernel(offsets, distances, scales, screen, moved, tables, phasors):
    del moved
    device = lax.axis_index(AXES)
    transfer_table(tables, 0, distances[0], offsets[0])
    transfer_table(tables, 1, distances[1], jnp.int32(0))

    def tiles(j, carry):
        for i in range(4):
            n1 = 4 * j + i
            lanes = pl.ds(pl.multiple_of(n1 * LANES, LANES), LANES)
            scale = scales[device // 4, n1] * (0.5 / math.pi)
            phasors[0, :, lanes], phasors[1, :, lanes] = phasor(
                screen[:, lanes].astype(F32) * scale
            )
        return carry

    lax.fori_loop(0, 8, tiles, 0)


def columns_kernel(
    arrived_in, tables_in, twiddle_in, weight_in, moved,
    field, l0, l1, l2, l3, r0, r1, r2, r3,
    turned, arrived, tables, twiddle, weight, blocks, arrival, departure,
):
    constants = [
        pltpu.make_async_copy(source, target, arrival.at[33 + i])
        for i, (source, target) in enumerate(
            ((tables_in, tables), (twiddle_in, twiddle), (weight_in, weight))
        )
    ]

    def copy_of(n1):
        part = slice(4 * n1, 4 * n1 + 4), slice(0, 32)
        if n1 == 32:
            part = slice(0, 128), slice(32, 64)
        return pltpu.make_async_copy(arrived_in.at[part], arrived.at[part], arrival.at[n1])

    for b in range(8):
        for a in range(4):
            copy_of(8 * a + b).start()
    for copy in constants:
        copy.start()
    copy_of(32).start()

    def leaving(n1):
        rows = slice(n1 * LANES, (n1 + 1) * LANES)
        return pltpu.make_async_copy(blocks.at[rows], moved.at[rows], departure.at[n1])

    def turned_rows(slot, g):
        return turned.at[slot, 8 * g : 8 * g + 8], turned.at[slot, 8 * g + 64 : 8 * g + 72]

    for b in range(8):
        slots = [a + 4 * (b % 2) for a in range(4)]
        for a in range(4):
            copy_of(8 * a + b).wait()
        for a in range(4):
            n1 = 8 * a + b
            turned[slots[a]] = arrived[4 * n1 : 4 * n1 + 4, :32].reshape((LANES, LANES)).T
        for g in range(8):
            x = []
            for slot in slots:
                real, imag = turned_rows(slot, g)
                x.append((real[...], imag[...]))
            enter(field, b, slice(8 * g, 8 * g + 8), x + [None] * 4)

    for copy in constants:
        copy.wait()
    buffers = (l0, l1, l2, l3), (r0, r1, r2, r3)
    spectral_pass(field, (tables, 0), twiddle, weight, *buffers, 64)
    copy_of(32).wait()
    low = low_half((8, LANES))

    def middle(g, carry):
        for half in range(2):
            rows = eight_rows(g + 4 * half)
            packed = eight_rows(g + 4)
            for b in range(8):
                x = leave(field, b, rows)
                for a in range(8):
                    n1 = 8 * a + b
                    even, odd = arrived[2 * n1, packed], arrived[2 * n1 + 1, packed]
                    x[a] = c_mul(x[a], phasor(swap_halves(even, odd, low)[half]))
                enter(field, b, rows, x)
        return carry

    lax.fori_loop(0, 4, middle, 0)
    spectral_pass(field, (tables, 1), twiddle, weight, *buffers, 64)

    for b in range(8):
        slots = [a + 4 * (b % 2) for a in range(4)]
        for g in range(8):
            x = leave(field, b, slice(8 * g, 8 * g + 8))
            for a in range(4):
                real, imag = turned_rows(slots[a], g)
                real[...], imag[...] = x[a + 2]
        for a in range(4):
            n1 = 8 * a + b
            blocks[n1 * LANES : (n1 + 1) * LANES, :] = turned[slots[a]].T
            leaving(n1).start()
    for n1 in range(32):
        leaving(n1).wait()


def last_rows_kernel(
    arrived, tables, phasors, twiddle, weight, output_in_hbm,
    field, l0, l1, l2, l3, r0, r1, r2, r3, output, departure,
):
    low = low_half((8, LANES))

    def first(g, carry):
        rows = eight_rows(g)
        for b in range(8):
            x = []
            for a in range(8):
                n1 = 8 * a + b
                x.append(swap_halves(arrived[2 * n1, rows], arrived[2 * n1 + 1, rows], low))
            enter(field, b, rows, x)
        return carry

    lax.fori_loop(0, 4, first, 0)
    spectral_pass(field, (tables, 1), twiddle, weight, (l0, l1, l2, l3), (r0, r1, r2, r3), 32)

    def last(g, carry):
        rows = eight_rows(g)
        for b in range(8):
            x = leave(field, b, rows)
            for a in range(4):
                n1 = 8 * a + b
                lanes = slice(n1 * LANES, (n1 + 1) * LANES)
                value = c_mul(x[a + 2], (phasors[0, rows, lanes], phasors[1, rows, lanes]))
                output[0, rows, lanes] = value[0]
                output[1, rows, lanes] = value[1]
        leaving(g).start()
        return carry

    def leaving(g):
        rows = eight_rows(g)
        return pltpu.make_async_copy(
            output.at[:, rows], output_in_hbm.at[:, rows], departure.at[g]
        )

    lax.fori_loop(0, 4, last, 0)
    for g in range(4):
        leaving(g).wait()


def call(kernel, kinds, shapes, batch, extra, flops, out_kind="v", limit=40):
    space = {"s": pltpu.SMEM, "v": pltpu.VMEM, "h": pltpu.HBM}
    scratch = [
        pltpu.VMEM((2, 8, 8, batch, LANES), F32),
        *[pltpu.VMEM((512, 4 * LANES), BF16)] * 4,
        *[pltpu.VMEM((512, 2 * LANES), F32)] * 4,
    ] if batch else []
    return pl.pallas_call(
        kernel,
        out_shape=[jax.ShapeDtypeStruct(shape, F32) for shape in shapes],
        in_specs=[pl.BlockSpec(memory_space=space[kind]) for kind in kinds],
        out_specs=[pl.BlockSpec(memory_space=space[out_kind]) for _ in shapes],
        scratch_shapes=scratch + extra,
        compiler_params=pltpu.CompilerParams(vmem_limit_bytes=limit << 20),
        cost_estimate=pl.CostEstimate(flops=flops, bytes_accessed=4 << 20, transcendentals=0),
    )


def exchange(blocks):
    return lax.all_to_all(blocks, AXES, split_axis=0, concat_axis=0, tiled=True)


def body(input_beam, offsets, distances, screens, screen_scales, last_screen, last_scales):
    twiddle, weight = (jnp.asarray(array) for array in constant_tables())
    table = (2, 8, 8, LANES)
    extra = [
        pltpu.VMEM((1, *table), F32),
        pltpu.SMEM((2,), jnp.int32),
        pltpu.SMEM((2,), F32),
        pltpu.SMEM((1, 64, 64), F32),
        pltpu.VMEM((2, 32, 4096), F32),
        pltpu.VMEM((1, 64, N), jnp.int32),
        pltpu.VMEM(twiddle.shape, F32),
        pltpu.VMEM(weight.shape, BF16),
        pltpu.VMEM((128, 64, LANES), F32),
        pltpu.SemaphoreType.DMA((7,)),
        pltpu.SemaphoreType.DMA((5,)),
    ]
    (moved,) = call(
        first_rows_kernel, "hhhhhhh", [(128, 64, LANES)], 32, extra, 10**10, "h", 60
    )(offsets, distances, screen_scales, input_beam, screens, twiddle, weight)
    tables, phasors = call(
        tables_kernel, "sssvh", [(2, *table), (2, 32, 4096)], 0, [], 10**9, "v", 60
    )(offsets, distances, last_scales, last_screen, moved)
    extra = [
        pltpu.VMEM((8, LANES, LANES), F32),
        pltpu.VMEM((128, 64, LANES), F32),
        pltpu.VMEM((2, *table), F32),
        pltpu.VMEM(twiddle.shape, F32),
        pltpu.VMEM(weight.shape, BF16),
        pltpu.VMEM((4096, LANES), F32),
        pltpu.SemaphoreType.DMA((36,)),
        pltpu.SemaphoreType.DMA((32,)),
    ]
    (moved,) = call(
        columns_kernel, "hhhh", [(4096, LANES)], 64, extra, 4 * 10**10, "h", 60
    )(exchange(moved), tables, twiddle, weight)
    arrived = exchange(moved.reshape((128, 32, LANES)))
    extra = [pltpu.VMEM((2, 32, 4096), F32), pltpu.SemaphoreType.DMA((4,))]
    (output,) = call(last_rows_kernel, "vvvvv", [(2, 32, 4096)], 32, extra, 10**10, "h")(
        arrived, tables, phasors, twiddle, weight
    )
    return output


def solution(mesh):
    return jax.shard_map(
        body,
        mesh=mesh,
        in_specs=(
            P(None, AXES, None),
            P(),
            P(),
            P(None, AXES, None),
            P(),
            P(AXES, None),
            P(),
        ),
        out_specs=P(None, AXES, None),
        check_vma=False,
    )
```

```python
import math

import jax
import jax.numpy as jnp
import numpy as np
from jax import lax
from jax.experimental import pallas as pl
from jax.experimental.pallas import tpu as pltpu
from jax.sharding import PartitionSpec as P

N = 8192
LANES = 128
AXES = ("gx", "gy")
ROOT_HALF = math.sqrt(0.5)
SINE = [
    math.sqrt(2.0) * term
    for term in (3.14159264013, -5.16771008351, 2.55007752321, -0.598291285620, 0.0776576603045)
]
COSINE = [
    math.sqrt(2.0) * term
    for term in (0.999999953248, -4.93479283062, 4.05841135286, -1.33187656808, 0.219689611098)
]
F32 = jnp.float32
BF16 = jnp.bfloat16


def constant_tables():
    k1 = np.arange(8)[:, None] + 8 * np.arange(8)[None, :]
    angle = -2.0 * np.pi * (k1[:, :, None] * np.arange(LANES)[None, None, :]) / N
    twiddle = np.stack([np.cos(angle), np.sin(angle)]).astype(np.float32)
    lane = np.arange(LANES)
    angle = -2.0 * np.pi * ((lane[:, None] * lane[None, :]) % LANES) / LANES
    cosine, sine = np.cos(angle), np.sin(angle)
    full = np.block([[cosine, sine], [-sine, cosine]]).astype(np.float32)
    high = full.astype(jnp.bfloat16)
    low = (full - high.astype(np.float32)).astype(jnp.bfloat16)
    return twiddle, np.concatenate([high, high, low])


def c_add(x, y):
    if x is None:
        return y
    if y is None:
        return x
    return (x[0] + y[0], x[1] + y[1])


def c_sub(x, y):
    if y is None:
        return x
    if x is None:
        return (-y[0], -y[1])
    return (x[0] - y[0], x[1] - y[1])


def c_mul(x, y):
    return (x[0] * y[0] - x[1] * y[1], x[0] * y[1] + x[1] * y[0])


def c_mul_conj(x, y):
    return (x[0] * y[0] + x[1] * y[1], x[1] * y[0] - x[0] * y[1])


def turn(x, sign):
    if x is None:
        return None
    return (-x[1], x[0]) if sign > 0 else (x[1], -x[0])


def eighth(x, sign):
    if x is None:
        return None
    if sign > 0:
        return ((x[0] - x[1]) * ROOT_HALF, (x[1] + x[0]) * ROOT_HALF)
    return ((x[0] + x[1]) * ROOT_HALF, (x[1] - x[0]) * ROOT_HALF)


def radix4(x0, x1, x2, x3, sign):
    even_sum, even_diff = c_add(x0, x2), c_sub(x0, x2)
    odd_sum, odd_diff = c_add(x1, x3), turn(c_sub(x1, x3), sign)
    return [
        c_add(even_sum, odd_sum),
        c_add(even_diff, odd_diff),
        c_sub(even_sum, odd_sum),
        c_sub(even_diff, odd_diff),
    ]


def radix8(x, sign):
    even = radix4(x[0], x[2], x[4], x[6], sign)
    odd = radix4(x[1], x[3], x[5], x[7], sign)
    odd[1] = eighth(odd[1], sign)
    odd[2] = turn(odd[2], sign)
    odd[3] = turn(eighth(odd[3], sign), sign)
    return [c_add(even[i], odd[i]) for i in range(4)] + [
        c_sub(even[i], odd[i]) for i in range(4)
    ]


def unit_root(x, index, sign):
    index = index % 64
    if index == 0:
        return x
    if index == 8:
        return eighth(x, sign)
    if index == 16:
        return turn(x, sign)
    angle = 2.0 * math.pi * index / 64
    return c_mul(x, (math.cos(angle), sign * math.sin(angle)))


def sincos(angle):
    turns = jnp.floor(angle * (2.0 / math.pi) + 0.5)
    rest = angle - turns * 1.5703125
    rest = rest - turns * 4.837512969970703125e-4
    rest = rest - turns * 7.54978995489188216e-8
    square = rest * rest
    sine = rest + rest * square * (
        -1.6666654611e-1 + square * (8.3321608736e-3 - square * 1.9515295891e-4)
    )
    cosine = (
        1.0
        - 0.5 * square
        + square
        * square
        * (4.166664568298827e-2 + square * (-1.388731625493765e-3 + square * 2.443315711809948e-5))
    )
    quarter = turns.astype(jnp.int32)
    swap = (quarter & 1) == 1
    sin_part = jnp.where(swap, cosine, sine)
    cos_part = jnp.where(swap, sine, cosine)
    sin_out = jnp.where((quarter & 2) == 2, -sin_part, sin_part)
    cos_out = jnp.where(((quarter + 1) & 2) == 2, -cos_part, cos_part)
    return cos_out, sin_out


def phasor(turns):
    rest = turns - jnp.floor(turns + 0.5)
    square = rest * rest
    sine = rest * (
        SINE[0]
        + square * (SINE[1] + square * (SINE[2] + square * (SINE[3] + square * SINE[4])))
    )
    cosine = COSINE[0] + square * (
        COSINE[1] + square * (COSINE[2] + square * (COSINE[3] + square * COSINE[4]))
    )
    return 1.0 - sine * sine, sine * cosine


def transfer_table(table, at, distance, offset):
    shape = (8, LANES)
    q_ids = lax.broadcasted_iota(jnp.int32, shape, 0)
    lane_ids = lax.broadcasted_iota(jnp.int32, shape, 1)
    coef = jnp.full(shape, distance, F32) * ((2.0 * math.pi / N) ** 2)
    coef1 = coef.astype(BF16).astype(F32)
    coef2 = (coef - coef1).astype(BF16).astype(F32)
    coef3 = (coef - coef1) - coef2
    for p in range(8):
        k = p + 8 * q_ids + 64 * lane_ids
        k = jnp.where(k < N // 2, k, k - N)
        squared = k * k
        upper = (squared & ~4095).astype(F32)
        lower = (squared & 4095).astype(F32)
        top = coef1 * upper
        turns = jnp.floor(top * (0.5 / math.pi) + 0.5)
        rest = (top - turns * 6.28125) - turns * 1.9350051879882812e-3
        rest = rest - turns * 3.0199159819567529e-7
        rest = rest + (coef2 * upper + (coef1 * lower + (coef3 * upper + coef2 * lower)))
        ramp = (k * offset) & (N - 1)
        ramp = jnp.where(ramp < N // 2, ramp, ramp - N).astype(F32) * (2.0 * math.pi / N)
        cosine, sine = sincos(rest + ramp)
        table[at, 0, p] = cosine * (1.0 / N)
        table[at, 1, p] = sine * (-1.0 / N)


def store_split(lhs, row, values):
    for i, (first, second) in enumerate(values):
        both = jnp.concatenate([first, second], axis=1)
        high = both.astype(BF16)
        low = (both - high.astype(F32)).astype(BF16)
        rows = slice(row + 8 * i, row + 8 * i + 8)
        lhs[rows, : 2 * LANES] = high
        lhs[rows, 2 * LANES :] = low


def product(lhs, weight):
    high, low = lhs[:, : 2 * LANES], lhs[:, 2 * LANES :]
    return jnp.dot(
        jnp.concatenate([high, low, high], axis=1), weight[...], preferred_element_type=F32
    )


def spectral_pass(field, table, twiddle, weight, left, result, batch, side=None):
    groups = batch // 8
    width = 2
    steps = 8 // width

    def row_of(values, part, p, q):
        return values[part, p, q : q + 1, :]

    def table_row(part, p, q):
        values, at = table
        return values[at, part, p, q : q + 1, :]

    def places(step):
        for j in range(width):
            for g in range(groups):
                yield step * width + j, slice(8 * g, 8 * g + 8), 64 * (groups * j + g)

    def result_rows(row, q):
        return slice(row + 8 * q, row + 8 * q + 8)

    def forward(step, lhs):
        for i, (p, rows, row) in enumerate(places(step)):
            if side is not None:
                side(step, i)
            x = radix8([(field[0, p, b, rows], field[1, p, b, rows]) for b in range(8)], -1)
            x = [
                c_mul(x[q], (row_of(twiddle, 0, p, q), row_of(twiddle, 1, p, q)))
                for q in range(8)
            ]
            store_split(lhs, row, x)

    def transfer(step, values, lhs):
        for p, rows, row in places(step):
            x = []
            for q in range(8):
                at = result_rows(row, q)
                value = (values[at, :LANES], values[at, LANES:])
                x.append(c_mul(value, (table_row(0, p, q), table_row(1, p, q))))
            store_split(lhs, row, [(v[1], v[0]) for v in x])

    def inverse(step, values):
        for p, rows, row in places(step):
            x = []
            for q in range(8):
                at = result_rows(row, q)
                value = (values[at, LANES:], values[at, :LANES])
                x.append(
                    c_mul_conj(value, (row_of(twiddle, 0, p, q), row_of(twiddle, 1, p, q)))
                )
            x = radix8(x, 1)
            for b in range(8):
                field[0, p, b, rows] = x[b][0]
                field[1, p, b, rows] = x[b][1]

    def multiply(lhs, values):
        values[...] = product(lhs, weight)

    forward_left, inverse_left = left[:2], left[2:]
    forward_result, inverse_result = result[:2], result[2:]
    forward(0, forward_left[0])
    multiply(forward_left[0], forward_result[0])
    forward(1, forward_left[1])
    multiply(forward_left[1], forward_result[1])
    transfer(0, forward_result[0], inverse_left[0])
    multiply(inverse_left[0], inverse_result[0])
    forward(2, forward_left[0])

    def two_steps(step):
        multiply(forward_left[0], forward_result[0])
        transfer(step - 1, forward_result[1], inverse_left[1])
        multiply(inverse_left[1], inverse_result[1])
        inverse(step - 2, inverse_result[0])
        forward(step + 1, forward_left[1])
        multiply(forward_left[1], forward_result[1])
        transfer(step, forward_result[0], inverse_left[0])
        multiply(inverse_left[0], inverse_result[0])
        inverse(step - 1, inverse_result[1])

    two_steps(2)
    transfer(steps - 1, forward_result[1], inverse_left[1])
    multiply(inverse_left[1], inverse_result[1])
    inverse(steps - 2, inverse_result[0])
    inverse(steps - 1, inverse_result[1])


def enter(field, b, rows, x):
    x = radix8(x, -1)
    for p in range(8):
        value = unit_root(x[p], b * p, -1)
        field[0, p, b, rows] = value[0]
        field[1, p, b, rows] = value[1]


def leave(field, b, rows):
    x = [unit_root((field[0, p, b, rows], field[1, p, b, rows]), b * p, 1) for p in range(8)]
    return radix8(x, 1)


def low_half(shape):
    return lax.broadcasted_iota(jnp.int32, shape, len(shape) - 1) < LANES // 2


def swap_halves(even, odd, low):
    crossed = pltpu.roll(jnp.where(low, odd, even), LANES // 2, 1)
    return jnp.where(low, even, crossed), jnp.where(low, crossed, odd)


def eight_rows(g):
    return pl.ds(pl.multiple_of(g * 8, 8), 8)


def pack_screen(j, scales, screen, moved, device, low):
    tiles = []
    for half in range(2):
        start = j * (2 * LANES) + half * LANES
        lanes = pl.ds(start if isinstance(j, int) else pl.multiple_of(start, LANES), LANES)
        scale = scales[0, device // 2, 2 * j + half] * (0.5 / math.pi)
        tiles.append(screen[0, :, lanes].astype(F32) * scale)
    block = jnp.concatenate(tiles, axis=0).T
    for half in range(2):
        part = block[64 * half : 64 * half + 64]
        first, second = swap_halves(part[:32], part[32:], low)
        moved[4 * j + half, 32:] = first
        moved[4 * j + 2 + half, 32:] = second


def first_rows_kernel(
    offsets_in, distances_in, scales_in, beam_in, screen_in, twiddle_in, weight_in, moved,
    field, l0, l1, l2, l3, r0, r1, r2, r3, table,
    offsets, distances, scales, beam, screen, twiddle, weight, blocks, arrival, departure,
):
    pairs = (
        (offsets_in, offsets), (distances_in, distances), (scales_in, scales),
        (beam_in, beam), (twiddle_in, twiddle), (weight_in, weight), (screen_in, screen),
    )
    copies = [
        pltpu.make_async_copy(source, target, arrival.at[i])
        for i, (source, target) in enumerate(pairs)
    ]
    for copy in copies:
        copy.start()
    device = lax.axis_index(AXES)
    for copy in copies[:2]:
        copy.wait()
    transfer_table(table, 0, distances[0], offsets[1])
    copies[3].wait()

    def leaving(part):
        rows = slice(32, 64) if part == 4 else slice(8 * part, 8 * part + 8)
        return pltpu.make_async_copy(blocks.at[:, rows], moved.at[:, rows], departure.at[part])

    low = low_half((8, LANES))

    def first(g):
        rows = slice(8 * g, 8 * g + 8)
        for b in range(8):
            x = []
            for a in range(8):
                n1 = 8 * a + b
                lanes = slice(n1 * LANES, (n1 + 1) * LANES)
                x.append((beam[0, rows, lanes], beam[1, rows, lanes]) if a < 4 else None)
            enter(field, b, rows, x)

    for g in range(4):
        first(g)
    for copy in (copies[2], *copies[4:]):
        copy.wait()
    low_packed = low_half((32, LANES))
    spectral_pass(
        field, (table, 0), twiddle, weight, (l0, l1, l2, l3), (r0, r1, r2, r3), 32,
        lambda step, i: pack_screen(8 * step + i, scales, screen, blocks, device, low_packed),
    )
    leaving(4).start()

    def last(g):
        rows = slice(8 * g, 8 * g + 8)
        for b in range(8):
            x = leave(field, b, rows)
            for a in range(8):
                n1 = 8 * a + b
                even, odd = swap_halves(x[a][0], x[a][1], low)
                blocks[2 * n1, rows] = even
                blocks[2 * n1 + 1, rows] = odd
        leaving(g).start()

    for g in range(4):
        last(g)
    for part in range(5):
        leaving(part).wait()


def tables_kernel(offsets, distances, scales, screen, moved, tables, phasors):
    del moved
    device = lax.axis_index(AXES)
    transfer_table(tables, 0, distances[0], offsets[0])
    transfer_table(tables, 1, distances[1], jnp.int32(0))

    def tiles(j, carry):
        for i in range(4):
            n1 = 4 * j + i
            lanes = pl.ds(pl.multiple_of(n1 * LANES, LANES), LANES)
            scale = scales[device // 4, n1] * (0.5 / math.pi)
            phasors[0, :, lanes], phasors[1, :, lanes] = phasor(
                screen[:, lanes].astype(F32) * scale
            )
        return carry

    lax.fori_loop(0, 8, tiles, 0)


def columns_kernel(
    arrived_in, tables_in, twiddle_in, weight_in, moved,
    field, l0, l1, l2, l3, r0, r1, r2, r3,
    turned, arrived, tables, twiddle, weight, blocks, arrival, departure,
):
    constants = [
        pltpu.make_async_copy(source, target, arrival.at[33 + i])
        for i, (source, target) in enumerate(
            ((tables_in, tables), (twiddle_in, twiddle), (weight_in, weight))
        )
    ]

    def copy_of(n1):
        part = slice(4 * n1, 4 * n1 + 4), slice(0, 32)
        if n1 == 32:
            part = slice(0, 128), slice(32, 64)
        return pltpu.make_async_copy(arrived_in.at[part], arrived.at[part], arrival.at[n1])

    for b in range(8):
        for a in range(4):
            copy_of(8 * a + b).start()
    for copy in constants:
        copy.start()
    copy_of(32).start()

    def leaving(n1):
        rows = slice(n1 * LANES, (n1 + 1) * LANES)
        return pltpu.make_async_copy(blocks.at[rows], moved.at[rows], departure.at[n1])

    def turned_rows(slot, g):
        return turned.at[slot, 8 * g : 8 * g + 8], turned.at[slot, 8 * g + 64 : 8 * g + 72]

    for b in range(8):
        slots = [a + 4 * (b % 2) for a in range(4)]
        for a in range(4):
            copy_of(8 * a + b).wait()
        for a in range(4):
            n1 = 8 * a + b
            turned[slots[a]] = arrived[4 * n1 : 4 * n1 + 4, :32].reshape((LANES, LANES)).T
        for g in range(8):
            x = []
            for slot in slots:
                real, imag = turned_rows(slot, g)
                x.append((real[...], imag[...]))
            enter(field, b, slice(8 * g, 8 * g + 8), x + [None] * 4)

    for copy in constants:
        copy.wait()
    buffers = (l0, l1, l2, l3), (r0, r1, r2, r3)
    spectral_pass(field, (tables, 0), twiddle, weight, *buffers, 64)
    copy_of(32).wait()
    low = low_half((8, LANES))

    def middle(g, carry):
        for half in range(2):
            rows = eight_rows(g + 4 * half)
            packed = eight_rows(g + 4)
            for b in range(8):
                x = leave(field, b, rows)
                for a in range(8):
                    n1 = 8 * a + b
                    even, odd = arrived[2 * n1, packed], arrived[2 * n1 + 1, packed]
                    if half == 0:
                        turns = jnp.where(low, even, pltpu.roll(odd, LANES // 2, 1))
                    else:
                        turns = jnp.where(low, pltpu.roll(even, LANES // 2, 1), odd)
                    x[a] = c_mul(x[a], phasor(turns))
                enter(field, b, rows, x)
        return carry

    lax.fori_loop(0, 4, middle, 0)
    spectral_pass(field, (tables, 1), twiddle, weight, *buffers, 64)

    for b in range(8):
        slots = [a + 4 * (b % 2) for a in range(4)]
        for g in range(8):
            x = leave(field, b, slice(8 * g, 8 * g + 8))
            for a in range(4):
                real, imag = turned_rows(slots[a], g)
                real[...], imag[...] = x[a + 2]
        for a in range(4):
            n1 = 8 * a + b
            blocks[n1 * LANES : (n1 + 1) * LANES, :] = turned[slots[a]].T
            leaving(n1).start()
    for n1 in range(32):
        leaving(n1).wait()


def last_rows_kernel(
    arrived, tables, phasors, twiddle, weight, output_in_hbm,
    field, l0, l1, l2, l3, r0, r1, r2, r3, output, departure,
):
    low = low_half((8, LANES))

    def first(g):
        rows = slice(8 * g, 8 * g + 8)
        for b in range(8):
            x = []
            for a in range(8):
                n1 = 8 * a + b
                x.append(swap_halves(arrived[2 * n1, rows], arrived[2 * n1 + 1, rows], low))
            enter(field, b, rows, x)

    for g in range(4):
        first(g)
    spectral_pass(field, (tables, 1), twiddle, weight, (l0, l1, l2, l3), (r0, r1, r2, r3), 32)

    def last(g):
        rows = slice(8 * g, 8 * g + 8)
        for b in range(8):
            x = leave(field, b, rows)
            for a in range(4):
                n1 = 8 * a + b
                lanes = slice(n1 * LANES, (n1 + 1) * LANES)
                value = c_mul(x[a + 2], (phasors[0, rows, lanes], phasors[1, rows, lanes]))
                output[0, rows, lanes] = value[0]
                output[1, rows, lanes] = value[1]
        leaving(g).start()

    def leaving(g):
        rows = slice(8 * g, 8 * g + 8)
        return pltpu.make_async_copy(
            output.at[:, rows], output_in_hbm.at[:, rows], departure.at[g]
        )

    for g in range(4):
        last(g)
    for g in range(4):
        leaving(g).wait()


def call(kernel, kinds, shapes, batch, extra, flops, out_kind="v", limit=40):
    space = {"s": pltpu.SMEM, "v": pltpu.VMEM, "h": pltpu.HBM}
    scratch = [
        pltpu.VMEM((2, 8, 8, batch, LANES), F32),
        *[pltpu.VMEM((16 * batch, 4 * LANES), BF16)] * 4,
        *[pltpu.VMEM((16 * batch, 2 * LANES), F32)] * 4,
    ] if batch else []
    return pl.pallas_call(
        kernel,
        out_shape=[jax.ShapeDtypeStruct(shape, F32) for shape in shapes],
        in_specs=[pl.BlockSpec(memory_space=space[kind]) for kind in kinds],
        out_specs=[pl.BlockSpec(memory_space=space[out_kind]) for _ in shapes],
        scratch_shapes=scratch + extra,
        compiler_params=pltpu.CompilerParams(vmem_limit_bytes=limit << 20),
        cost_estimate=pl.CostEstimate(flops=flops, bytes_accessed=4 << 20, transcendentals=0),
    )


def exchange(blocks):
    return lax.all_to_all(blocks, AXES, split_axis=0, concat_axis=0, tiled=True)


def body(input_beam, offsets, distances, screens, screen_scales, last_screen, last_scales):
    twiddle, weight = (jnp.asarray(array) for array in constant_tables())
    table = (2, 8, 8, LANES)
    extra = [
        pltpu.VMEM((1, *table), F32),
        pltpu.SMEM((2,), jnp.int32),
        pltpu.SMEM((2,), F32),
        pltpu.SMEM((1, 64, 64), F32),
        pltpu.VMEM((2, 32, 4096), F32),
        pltpu.VMEM((1, 64, N), jnp.int32),
        pltpu.VMEM(twiddle.shape, F32),
        pltpu.VMEM(weight.shape, BF16),
        pltpu.VMEM((128, 64, LANES), F32),
        pltpu.SemaphoreType.DMA((7,)),
        pltpu.SemaphoreType.DMA((5,)),
    ]
    (moved,) = call(
        first_rows_kernel, "hhhhhhh", [(128, 64, LANES)], 32, extra, 10**10, "h", 60
    )(offsets, distances, screen_scales, input_beam, screens, twiddle, weight)
    tables, phasors = call(
        tables_kernel, "sssvh", [(2, *table), (2, 32, 4096)], 0, [], 10**9, "v", 60
    )(offsets, distances, last_scales, last_screen, moved)
    extra = [
        pltpu.VMEM((8, LANES, LANES), F32),
        pltpu.VMEM((128, 64, LANES), F32),
        pltpu.VMEM((2, *table), F32),
        pltpu.VMEM(twiddle.shape, F32),
        pltpu.VMEM(weight.shape, BF16),
        pltpu.VMEM((4096, LANES), F32),
        pltpu.SemaphoreType.DMA((36,)),
        pltpu.SemaphoreType.DMA((32,)),
    ]
    (moved,) = call(
        columns_kernel, "hhhh", [(4096, LANES)], 64, extra, 4 * 10**10, "h", 60
    )(exchange(moved), tables, twiddle, weight)
    arrived = exchange(moved.reshape((128, 32, LANES)))
    extra = [pltpu.VMEM((2, 32, 4096), F32), pltpu.SemaphoreType.DMA((4,))]
    (output,) = call(last_rows_kernel, "vvvvv", [(2, 32, 4096)], 32, extra, 10**10, "h")(
        arrived, tables, phasors, twiddle, weight
    )
    return output


def solution(mesh):
    return jax.shard_map(
        body,
        mesh=mesh,
        in_specs=(
            P(None, AXES, None),
            P(),
            P(),
            P(None, AXES, None),
            P(),
            P(AXES, None),
            P(),
        ),
        out_specs=P(None, AXES, None),
        check_vma=False,
    )
```

```python
import math

import jax
import jax.numpy as jnp
import numpy as np
from jax import lax
from jax.experimental import pallas as pl
from jax.experimental.pallas import tpu as pltpu
from jax.sharding import PartitionSpec as P

N = 8192
LANES = 128
AXES = ("gx", "gy")
ROOT_HALF = math.sqrt(0.5)
SINE = [
    math.sqrt(2.0) * term
    for term in (3.14159264013, -5.16771008351, 2.55007752321, -0.598291285620, 0.0776576603045)
]
COSINE = [
    math.sqrt(2.0) * term
    for term in (0.999999953248, -4.93479283062, 4.05841135286, -1.33187656808, 0.219689611098)
]
F32 = jnp.float32
BF16 = jnp.bfloat16


def constant_tables():
    k1 = np.arange(8)[:, None] + 8 * np.arange(8)[None, :]
    angle = -2.0 * np.pi * (k1[:, :, None] * np.arange(LANES)[None, None, :]) / N
    twiddle = np.stack([np.cos(angle), np.sin(angle)]).astype(np.float32)
    lane = np.arange(LANES)
    angle = -2.0 * np.pi * ((lane[:, None] * lane[None, :]) % LANES) / LANES
    cosine, sine = np.cos(angle), np.sin(angle)
    full = np.block([[cosine, sine], [-sine, cosine]]).astype(np.float32)
    high = full.astype(jnp.bfloat16)
    low = (full - high.astype(np.float32)).astype(jnp.bfloat16)
    return twiddle, np.concatenate([high, high, low])


def c_add(x, y):
    if x is None:
        return y
    if y is None:
        return x
    return (x[0] + y[0], x[1] + y[1])


def c_sub(x, y):
    if y is None:
        return x
    if x is None:
        return (-y[0], -y[1])
    return (x[0] - y[0], x[1] - y[1])


def c_mul(x, y):
    return (x[0] * y[0] - x[1] * y[1], x[0] * y[1] + x[1] * y[0])


def c_mul_conj(x, y):
    return (x[0] * y[0] + x[1] * y[1], x[1] * y[0] - x[0] * y[1])


def turn(x, sign):
    if x is None:
        return None
    return (-x[1], x[0]) if sign > 0 else (x[1], -x[0])


def eighth(x, sign):
    if x is None:
        return None
    if sign > 0:
        return ((x[0] - x[1]) * ROOT_HALF, (x[1] + x[0]) * ROOT_HALF)
    return ((x[0] + x[1]) * ROOT_HALF, (x[1] - x[0]) * ROOT_HALF)


def radix4(x0, x1, x2, x3, sign):
    even_sum, even_diff = c_add(x0, x2), c_sub(x0, x2)
    odd_sum, odd_diff = c_add(x1, x3), turn(c_sub(x1, x3), sign)
    return [
        c_add(even_sum, odd_sum),
        c_add(even_diff, odd_diff),
        c_sub(even_sum, odd_sum),
        c_sub(even_diff, odd_diff),
    ]


def radix8(x, sign):
    even = radix4(x[0], x[2], x[4], x[6], sign)
    odd = radix4(x[1], x[3], x[5], x[7], sign)
    odd[1] = eighth(odd[1], sign)
    odd[2] = turn(odd[2], sign)
    odd[3] = turn(eighth(odd[3], sign), sign)
    return [c_add(even[i], odd[i]) for i in range(4)] + [
        c_sub(even[i], odd[i]) for i in range(4)
    ]


def unit_root(x, index, sign):
    index = index % 64
    if index == 0:
        return x
    if index == 8:
        return eighth(x, sign)
    if index == 16:
        return turn(x, sign)
    angle = 2.0 * math.pi * index / 64
    return c_mul(x, (math.cos(angle), sign * math.sin(angle)))


def sincos(angle):
    turns = jnp.floor(angle * (2.0 / math.pi) + 0.5)
    rest = angle - turns * 1.5703125
    rest = rest - turns * 4.837512969970703125e-4
    rest = rest - turns * 7.54978995489188216e-8
    square = rest * rest
    sine = rest + rest * square * (
        -1.6666654611e-1 + square * (8.3321608736e-3 - square * 1.9515295891e-4)
    )
    cosine = (
        1.0
        - 0.5 * square
        + square
        * square
        * (4.166664568298827e-2 + square * (-1.388731625493765e-3 + square * 2.443315711809948e-5))
    )
    quarter = turns.astype(jnp.int32)
    swap = (quarter & 1) == 1
    sin_part = jnp.where(swap, cosine, sine)
    cos_part = jnp.where(swap, sine, cosine)
    sin_out = jnp.where((quarter & 2) == 2, -sin_part, sin_part)
    cos_out = jnp.where(((quarter + 1) & 2) == 2, -cos_part, cos_part)
    return cos_out, sin_out


def phasor(turns):
    rest = turns - jnp.floor(turns + 0.5)
    square = rest * rest
    sine = rest * (
        SINE[0]
        + square * (SINE[1] + square * (SINE[2] + square * (SINE[3] + square * SINE[4])))
    )
    cosine = COSINE[0] + square * (
        COSINE[1] + square * (COSINE[2] + square * (COSINE[3] + square * COSINE[4]))
    )
    return 1.0 - sine * sine, sine * cosine


def transfer_table(table, at, distance, offset):
    shape = (8, LANES)
    q_ids = lax.broadcasted_iota(jnp.int32, shape, 0)
    lane_ids = lax.broadcasted_iota(jnp.int32, shape, 1)
    coef = jnp.full(shape, distance, F32) * ((2.0 * math.pi / N) ** 2)
    coef1 = coef.astype(BF16).astype(F32)
    coef2 = (coef - coef1).astype(BF16).astype(F32)
    coef3 = (coef - coef1) - coef2
    for p in range(8):
        k = p + 8 * q_ids + 64 * lane_ids
        k = jnp.where(k < N // 2, k, k - N)
        squared = k * k
        upper = (squared & ~4095).astype(F32)
        lower = (squared & 4095).astype(F32)
        top = coef1 * upper
        turns = jnp.floor(top * (0.5 / math.pi) + 0.5)
        rest = (top - turns * 6.28125) - turns * 1.9350051879882812e-3
        rest = rest - turns * 3.0199159819567529e-7
        rest = rest + (coef2 * upper + (coef1 * lower + (coef3 * upper + coef2 * lower)))
        ramp = (k * offset) & (N - 1)
        ramp = jnp.where(ramp < N // 2, ramp, ramp - N).astype(F32) * (2.0 * math.pi / N)
        cosine, sine = sincos(rest + ramp)
        table[at, 0, p] = cosine * (1.0 / N)
        table[at, 1, p] = sine * (-1.0 / N)


def store_split(lhs, row, values):
    for i, (first, second) in enumerate(values):
        both = jnp.concatenate([first, second], axis=1)
        high = both.astype(BF16)
        low = (both - high.astype(F32)).astype(BF16)
        rows = slice(row + 8 * i, row + 8 * i + 8)
        lhs[rows, : 2 * LANES] = high
        lhs[rows, 2 * LANES :] = low


def product(lhs, weight):
    high, low = lhs[:, : 2 * LANES], lhs[:, 2 * LANES :]
    return jnp.dot(
        jnp.concatenate([high, low, high], axis=1), weight[...], preferred_element_type=F32
    )


def spectral_pass(field, table, twiddle, weight, left, result, batch, side=None):
    groups = batch // 8
    width = 2
    steps = 8 // width

    def row_of(values, part, p, q):
        return values[part, p, q : q + 1, :]

    def table_row(part, p, q):
        values, at = table
        return values[at, part, p, q : q + 1, :]

    def places(step):
        for j in range(width):
            for g in range(groups):
                yield step * width + j, slice(8 * g, 8 * g + 8), 64 * (groups * j + g)

    def result_rows(row, q):
        return slice(row + 8 * q, row + 8 * q + 8)

    def forward(step, lhs):
        for p, rows, row in places(step):
            x = radix8([(field[0, p, b, rows], field[1, p, b, rows]) for b in range(8)], -1)
            x = [
                c_mul(x[q], (row_of(twiddle, 0, p, q), row_of(twiddle, 1, p, q)))
                for q in range(8)
            ]
            store_split(lhs, row, x)

    def other_work(turn, i):
        if side is not None and turn is not None:
            side(2 * groups * turn + i)

    def transfer(step, values, lhs):
        for i, (p, rows, row) in enumerate(places(step)):
            other_work((0, 1, 2, None)[step], i)
            x = []
            for q in range(8):
                at = result_rows(row, q)
                value = (values[at, :LANES], values[at, LANES:])
                x.append(c_mul(value, (table_row(0, p, q), table_row(1, p, q))))
            store_split(lhs, row, [(v[1], v[0]) for v in x])

    def inverse(step, values):
        for i, (p, rows, row) in enumerate(places(step)):
            other_work((None, 3, None, None)[step], i)
            x = []
            for q in range(8):
                at = result_rows(row, q)
                value = (values[at, LANES:], values[at, :LANES])
                x.append(
                    c_mul_conj(value, (row_of(twiddle, 0, p, q), row_of(twiddle, 1, p, q)))
                )
            x = radix8(x, 1)
            for b in range(8):
                field[0, p, b, rows] = x[b][0]
                field[1, p, b, rows] = x[b][1]

    def multiply(lhs, values):
        values[...] = product(lhs, weight)

    forward_left, inverse_left = left[:2], left[2:]
    forward_result, inverse_result = result[:2], result[2:]
    forward(0, forward_left[0])
    multiply(forward_left[0], forward_result[0])
    forward(1, forward_left[1])
    multiply(forward_left[1], forward_result[1])
    transfer(0, forward_result[0], inverse_left[0])
    multiply(inverse_left[0], inverse_result[0])
    forward(2, forward_left[0])

    def two_steps(step):
        multiply(forward_left[0], forward_result[0])
        transfer(step - 1, forward_result[1], inverse_left[1])
        multiply(inverse_left[1], inverse_result[1])
        inverse(step - 2, inverse_result[0])
        forward(step + 1, forward_left[1])
        multiply(forward_left[1], forward_result[1])
        transfer(step, forward_result[0], inverse_left[0])
        multiply(inverse_left[0], inverse_result[0])
        inverse(step - 1, inverse_result[1])

    two_steps(2)
    transfer(steps - 1, forward_result[1], inverse_left[1])
    multiply(inverse_left[1], inverse_result[1])
    inverse(steps - 2, inverse_result[0])
    inverse(steps - 1, inverse_result[1])


def enter(field, b, rows, x):
    x = radix8(x, -1)
    for p in range(8):
        value = unit_root(x[p], b * p, -1)
        field[0, p, b, rows] = value[0]
        field[1, p, b, rows] = value[1]


def leave(field, b, rows):
    x = [unit_root((field[0, p, b, rows], field[1, p, b, rows]), b * p, 1) for p in range(8)]
    return radix8(x, 1)


def low_half(shape):
    return lax.broadcasted_iota(jnp.int32, shape, len(shape) - 1) < LANES // 2


def swap_halves(even, odd, low):
    crossed = pltpu.roll(jnp.where(low, odd, even), LANES // 2, 1)
    return jnp.where(low, even, crossed), jnp.where(low, crossed, odd)


def eight_rows(g):
    return pl.ds(pl.multiple_of(g * 8, 8), 8)


def pack_screen(j, scales, screen, moved, device, low):
    tiles = []
    for half in range(2):
        start = j * (2 * LANES) + half * LANES
        lanes = pl.ds(start if isinstance(j, int) else pl.multiple_of(start, LANES), LANES)
        scale = scales[0, device // 2, 2 * j + half] * (0.5 / math.pi)
        tiles.append(screen[0, :, lanes].astype(F32) * scale)
    block = jnp.concatenate(tiles, axis=0).T
    for half in range(2):
        part = block[64 * half : 64 * half + 64]
        first, second = swap_halves(part[:32], part[32:], low)
        moved[4 * j + half, 32:] = first
        moved[4 * j + 2 + half, 32:] = second


def first_rows_kernel(
    offsets_in, distances_in, scales_in, beam_in, screen_in, twiddle_in, weight_in, moved,
    field, l0, l1, l2, l3, r0, r1, r2, r3, table,
    offsets, distances, scales, beam, screen, twiddle, weight, blocks, arrival, departure,
):
    pairs = (
        (offsets_in, offsets), (distances_in, distances), (scales_in, scales),
        (beam_in, beam), (twiddle_in, twiddle), (weight_in, weight), (screen_in, screen),
    )
    copies = [
        pltpu.make_async_copy(source, target, arrival.at[i])
        for i, (source, target) in enumerate(pairs)
    ]
    for copy in copies:
        copy.start()
    device = lax.axis_index(AXES)
    for copy in copies[:2]:
        copy.wait()
    transfer_table(table, 0, distances[0], offsets[1])
    copies[3].wait()

    def leaving(part):
        rows = slice(32, 64) if part == 4 else slice(8 * part, 8 * part + 8)
        return pltpu.make_async_copy(blocks.at[:, rows], moved.at[:, rows], departure.at[part])

    low = low_half((8, LANES))

    def first(g):
        rows = slice(8 * g, 8 * g + 8)
        for b in range(8):
            x = []
            for a in range(8):
                n1 = 8 * a + b
                lanes = slice(n1 * LANES, (n1 + 1) * LANES)
                x.append((beam[0, rows, lanes], beam[1, rows, lanes]) if a < 4 else None)
            enter(field, b, rows, x)

    for g in range(4):
        first(g)
    for copy in (copies[2], *copies[4:]):
        copy.wait()
    low_packed = low_half((32, LANES))
    spectral_pass(
        field, (table, 0), twiddle, weight, (l0, l1, l2, l3), (r0, r1, r2, r3), 32,
        lambda j: pack_screen(j, scales, screen, blocks, device, low_packed),
    )
    leaving(4).start()

    def last(g):
        rows = slice(8 * g, 8 * g + 8)
        for b in range(8):
            x = leave(field, b, rows)
            for a in range(8):
                n1 = 8 * a + b
                even, odd = swap_halves(x[a][0], x[a][1], low)
                blocks[2 * n1, rows] = even
                blocks[2 * n1 + 1, rows] = odd
        leaving(g).start()

    for g in range(4):
        last(g)
    for part in range(5):
        leaving(part).wait()


def tables_kernel(offsets, distances, scales, screen, moved, tables, phasors):
    del moved
    device = lax.axis_index(AXES)
    transfer_table(tables, 0, distances[0], offsets[0])
    transfer_table(tables, 1, distances[1], jnp.int32(0))

    def tiles(j, carry):
        for i in range(4):
            n1 = 4 * j + i
            lanes = pl.ds(pl.multiple_of(n1 * LANES, LANES), LANES)
            scale = scales[device // 4, n1] * (0.5 / math.pi)
            phasors[0, :, lanes], phasors[1, :, lanes] = phasor(
                screen[:, lanes].astype(F32) * scale
            )
        return carry

    lax.fori_loop(0, 8, tiles, 0)


def columns_kernel(
    arrived_in, tables_in, twiddle_in, weight_in, moved,
    field, l0, l1, l2, l3, r0, r1, r2, r3,
    turned, arrived, factors, tables, twiddle, weight, blocks, arrival, departure,
):
    constants = [
        pltpu.make_async_copy(source, target, arrival.at[33 + i])
        for i, (source, target) in enumerate(
            ((tables_in, tables), (twiddle_in, twiddle), (weight_in, weight))
        )
    ]

    def copy_of(n1):
        part = slice(4 * n1, 4 * n1 + 4), slice(0, 32)
        if n1 == 32:
            part = slice(0, 128), slice(32, 64)
        return pltpu.make_async_copy(arrived_in.at[part], arrived.at[part], arrival.at[n1])

    for b in range(8):
        for a in range(4):
            copy_of(8 * a + b).start()
    for copy in constants:
        copy.start()
    copy_of(32).start()

    def leaving(n1):
        rows = slice(n1 * LANES, (n1 + 1) * LANES)
        return pltpu.make_async_copy(blocks.at[rows], moved.at[rows], departure.at[n1])

    def turned_rows(slot, g):
        return turned.at[slot, 8 * g : 8 * g + 8], turned.at[slot, 8 * g + 64 : 8 * g + 72]

    for b in range(8):
        slots = [a + 4 * (b % 2) for a in range(4)]
        for a in range(4):
            copy_of(8 * a + b).wait()
        for a in range(4):
            n1 = 8 * a + b
            turned[slots[a]] = arrived[4 * n1 : 4 * n1 + 4, :32].reshape((LANES, LANES)).T
        for g in range(8):
            x = []
            for slot in slots:
                real, imag = turned_rows(slot, g)
                x.append((real[...], imag[...]))
            enter(field, b, slice(8 * g, 8 * g + 8), x + [None] * 4)

    for copy in constants:
        copy.wait()
    copy_of(32).wait()
    buffers = (l0, l1, l2, l3), (r0, r1, r2, r3)
    low = low_half((32, LANES))

    def screen_factors(n1):
        halves = swap_halves(arrived[2 * n1, 32:], arrived[2 * n1 + 1, 32:], low)
        for half in range(2):
            rows = slice(32 * half, 32 * half + 32)
            factors[0, n1, rows], factors[1, n1, rows] = phasor(halves[half])

    spectral_pass(field, (tables, 0), twiddle, weight, *buffers, 64, screen_factors)

    def middle(g, carry):
        rows = eight_rows(g)
        for b in range(8):
            x = leave(field, b, rows)
            for a in range(8):
                n1 = 8 * a + b
                x[a] = c_mul(x[a], (factors[0, n1, rows], factors[1, n1, rows]))
            enter(field, b, rows, x)
        return carry

    lax.fori_loop(0, 8, middle, 0)
    spectral_pass(field, (tables, 1), twiddle, weight, *buffers, 64)

    for b in range(8):
        slots = [a + 4 * (b % 2) for a in range(4)]
        for g in range(8):
            x = leave(field, b, slice(8 * g, 8 * g + 8))
            for a in range(4):
                real, imag = turned_rows(slots[a], g)
                real[...], imag[...] = x[a + 2]
        for a in range(4):
            n1 = 8 * a + b
            blocks[n1 * LANES : (n1 + 1) * LANES, :] = turned[slots[a]].T
            leaving(n1).start()
    for n1 in range(32):
        leaving(n1).wait()


def last_rows_kernel(
    arrived, tables, phasors, twiddle, weight, output_in_hbm,
    field, l0, l1, l2, l3, r0, r1, r2, r3, output, departure,
):
    low = low_half((8, LANES))

    def first(g):
        rows = slice(8 * g, 8 * g + 8)
        for b in range(8):
            x = []
            for a in range(8):
                n1 = 8 * a + b
                x.append(swap_halves(arrived[2 * n1, rows], arrived[2 * n1 + 1, rows], low))
            enter(field, b, rows, x)

    for g in range(4):
        first(g)
    spectral_pass(field, (tables, 1), twiddle, weight, (l0, l1, l2, l3), (r0, r1, r2, r3), 32)

    def last(g):
        rows = slice(8 * g, 8 * g + 8)
        for b in range(8):
            x = leave(field, b, rows)
            for a in range(4):
                n1 = 8 * a + b
                lanes = slice(n1 * LANES, (n1 + 1) * LANES)
                value = c_mul(x[a + 2], (phasors[0, rows, lanes], phasors[1, rows, lanes]))
                output[0, rows, lanes] = value[0]
                output[1, rows, lanes] = value[1]
        leaving(g).start()

    def leaving(g):
        rows = slice(8 * g, 8 * g + 8)
        return pltpu.make_async_copy(
            output.at[:, rows], output_in_hbm.at[:, rows], departure.at[g]
        )

    for g in range(4):
        last(g)
    for g in range(4):
        leaving(g).wait()


def call(kernel, kinds, shapes, batch, extra, flops, out_kind="v", limit=40):
    space = {"s": pltpu.SMEM, "v": pltpu.VMEM, "h": pltpu.HBM}
    scratch = [
        pltpu.VMEM((2, 8, 8, batch, LANES), F32),
        *[pltpu.VMEM((16 * batch, 4 * LANES), BF16)] * 4,
        *[pltpu.VMEM((16 * batch, 2 * LANES), F32)] * 4,
    ] if batch else []
    return pl.pallas_call(
        kernel,
        out_shape=[jax.ShapeDtypeStruct(shape, F32) for shape in shapes],
        in_specs=[pl.BlockSpec(memory_space=space[kind]) for kind in kinds],
        out_specs=[pl.BlockSpec(memory_space=space[out_kind]) for _ in shapes],
        scratch_shapes=scratch + extra,
        compiler_params=pltpu.CompilerParams(vmem_limit_bytes=limit << 20),
        cost_estimate=pl.CostEstimate(flops=flops, bytes_accessed=4 << 20, transcendentals=0),
    )


def exchange(blocks):
    return lax.all_to_all(blocks, AXES, split_axis=0, concat_axis=0, tiled=True)


def body(input_beam, offsets, distances, screens, screen_scales, last_screen, last_scales):
    twiddle, weight = (jnp.asarray(array) for array in constant_tables())
    table = (2, 8, 8, LANES)
    extra = [
        pltpu.VMEM((1, *table), F32),
        pltpu.SMEM((2,), jnp.int32),
        pltpu.SMEM((2,), F32),
        pltpu.SMEM((1, 64, 64), F32),
        pltpu.VMEM((2, 32, 4096), F32),
        pltpu.VMEM((1, 64, N), jnp.int32),
        pltpu.VMEM(twiddle.shape, F32),
        pltpu.VMEM(weight.shape, BF16),
        pltpu.VMEM((128, 64, LANES), F32),
        pltpu.SemaphoreType.DMA((7,)),
        pltpu.SemaphoreType.DMA((5,)),
    ]
    (moved,) = call(
        first_rows_kernel, "hhhhhhh", [(128, 64, LANES)], 32, extra, 10**10, "h", 60
    )(offsets, distances, screen_scales, input_beam, screens, twiddle, weight)
    tables, phasors = call(
        tables_kernel, "sssvh", [(2, *table), (2, 32, 4096)], 0, [], 10**9, "v", 60
    )(offsets, distances, last_scales, last_screen, moved)
    extra = [
        pltpu.VMEM((8, LANES, LANES), F32),
        pltpu.VMEM((128, 64, LANES), F32),
        pltpu.VMEM((2, 64, 64, LANES), F32),
        pltpu.VMEM((2, *table), F32),
        pltpu.VMEM(twiddle.shape, F32),
        pltpu.VMEM(weight.shape, BF16),
        pltpu.VMEM((4096, LANES), F32),
        pltpu.SemaphoreType.DMA((36,)),
        pltpu.SemaphoreType.DMA((32,)),
    ]
    (moved,) = call(
        columns_kernel, "hhhh", [(4096, LANES)], 64, extra, 4 * 10**10, "h", 60
    )(exchange(moved), tables, twiddle, weight)
    arrived = exchange(moved.reshape((128, 32, LANES)))
    extra = [pltpu.VMEM((2, 32, 4096), F32), pltpu.SemaphoreType.DMA((4,))]
    (output,) = call(last_rows_kernel, "vvvvv", [(2, 32, 4096)], 32, extra, 10**10, "h")(
        arrived, tables, phasors, twiddle, weight
    )
    return output


def solution(mesh):
    return jax.shard_map(
        body,
        mesh=mesh,
        in_specs=(
            P(None, AXES, None),
            P(),
            P(),
            P(None, AXES, None),
            P(),
            P(AXES, None),
            P(),
        ),
        out_specs=P(None, AXES, None),
        check_vma=False,
    )
```

```python
import math

import jax
import jax.numpy as jnp
import numpy as np
from jax import lax
from jax.experimental import pallas as pl
from jax.experimental.pallas import tpu as pltpu
from jax.sharding import PartitionSpec as P

N = 8192
LANES = 128
AXES = ("gx", "gy")
ROOT_HALF = math.sqrt(0.5)
SINE = [
    math.sqrt(2.0) * term
    for term in (3.14159264013, -5.16771008351, 2.55007752321, -0.598291285620, 0.0776576603045)
]
COSINE = [
    math.sqrt(2.0) * term
    for term in (0.999999953248, -4.93479283062, 4.05841135286, -1.33187656808, 0.219689611098)
]
F32 = jnp.float32
BF16 = jnp.bfloat16


def constant_tables():
    k1 = np.arange(8)[:, None] + 8 * np.arange(8)[None, :]
    angle = -2.0 * np.pi * (k1[:, :, None] * np.arange(LANES)[None, None, :]) / N
    twiddle = np.stack([np.cos(angle), np.sin(angle)]).astype(np.float32)
    lane = np.arange(LANES)
    angle = -2.0 * np.pi * ((lane[:, None] * lane[None, :]) % LANES) / LANES
    cosine, sine = np.cos(angle), np.sin(angle)
    full = np.block([[cosine, sine], [-sine, cosine]]).astype(np.float32)
    high = full.astype(jnp.bfloat16)
    low = (full - high.astype(np.float32)).astype(jnp.bfloat16)
    return twiddle, np.concatenate([high, high, low])


def c_add(x, y):
    if x is None:
        return y
    if y is None:
        return x
    return (x[0] + y[0], x[1] + y[1])


def c_sub(x, y):
    if y is None:
        return x
    if x is None:
        return (-y[0], -y[1])
    return (x[0] - y[0], x[1] - y[1])


def c_mul(x, y):
    return (x[0] * y[0] - x[1] * y[1], x[0] * y[1] + x[1] * y[0])


def c_mul_conj(x, y):
    return (x[0] * y[0] + x[1] * y[1], x[1] * y[0] - x[0] * y[1])


def turn(x, sign):
    if x is None:
        return None
    return (-x[1], x[0]) if sign > 0 else (x[1], -x[0])


def eighth(x, sign):
    if x is None:
        return None
    if sign > 0:
        return ((x[0] - x[1]) * ROOT_HALF, (x[1] + x[0]) * ROOT_HALF)
    return ((x[0] + x[1]) * ROOT_HALF, (x[1] - x[0]) * ROOT_HALF)


def radix4(x0, x1, x2, x3, sign):
    even_sum, even_diff = c_add(x0, x2), c_sub(x0, x2)
    odd_sum, odd_diff = c_add(x1, x3), turn(c_sub(x1, x3), sign)
    return [
        c_add(even_sum, odd_sum),
        c_add(even_diff, odd_diff),
        c_sub(even_sum, odd_sum),
        c_sub(even_diff, odd_diff),
    ]


def radix8(x, sign):
    even = radix4(x[0], x[2], x[4], x[6], sign)
    odd = radix4(x[1], x[3], x[5], x[7], sign)
    odd[1] = eighth(odd[1], sign)
    odd[2] = turn(odd[2], sign)
    odd[3] = turn(eighth(odd[3], sign), sign)
    return [c_add(even[i], odd[i]) for i in range(4)] + [
        c_sub(even[i], odd[i]) for i in range(4)
    ]


def unit_root(x, index, sign):
    index = index % 64
    if index == 0:
        return x
    if index == 8:
        return eighth(x, sign)
    if index == 16:
        return turn(x, sign)
    angle = 2.0 * math.pi * index / 64
    return c_mul(x, (math.cos(angle), sign * math.sin(angle)))


def sincos(angle):
    turns = jnp.floor(angle * (2.0 / math.pi) + 0.5)
    rest = angle - turns * 1.5703125
    rest = rest - turns * 4.837512969970703125e-4
    rest = rest - turns * 7.54978995489188216e-8
    square = rest * rest
    sine = rest + rest * square * (
        -1.6666654611e-1 + square * (8.3321608736e-3 - square * 1.9515295891e-4)
    )
    cosine = (
        1.0
        - 0.5 * square
        + square
        * square
        * (4.166664568298827e-2 + square * (-1.388731625493765e-3 + square * 2.443315711809948e-5))
    )
    quarter = turns.astype(jnp.int32)
    swap = (quarter & 1) == 1
    sin_part = jnp.where(swap, cosine, sine)
    cos_part = jnp.where(swap, sine, cosine)
    sin_out = jnp.where((quarter & 2) == 2, -sin_part, sin_part)
    cos_out = jnp.where(((quarter + 1) & 2) == 2, -cos_part, cos_part)
    return cos_out, sin_out


def phasor(turns):
    rest = turns - jnp.floor(turns + 0.5)
    square = rest * rest
    sine = rest * (
        SINE[0]
        + square * (SINE[1] + square * (SINE[2] + square * (SINE[3] + square * SINE[4])))
    )
    cosine = COSINE[0] + square * (
        COSINE[1] + square * (COSINE[2] + square * (COSINE[3] + square * COSINE[4]))
    )
    return 1.0 - sine * sine, sine * cosine


def transfer_table(table, at, distance, offset):
    shape = (8, LANES)
    q_ids = lax.broadcasted_iota(jnp.int32, shape, 0)
    lane_ids = lax.broadcasted_iota(jnp.int32, shape, 1)
    coef = jnp.full(shape, distance, F32) * ((2.0 * math.pi / N) ** 2)
    coef1 = coef.astype(BF16).astype(F32)
    coef2 = (coef - coef1).astype(BF16).astype(F32)
    coef3 = (coef - coef1) - coef2
    for p in range(8):
        k = p + 8 * q_ids + 64 * lane_ids
        k = jnp.where(k < N // 2, k, k - N)
        squared = k * k
        upper = (squared & ~4095).astype(F32)
        lower = (squared & 4095).astype(F32)
        top = coef1 * upper
        turns = jnp.floor(top * (0.5 / math.pi) + 0.5)
        rest = (top - turns * 6.28125) - turns * 1.9350051879882812e-3
        rest = rest - turns * 3.0199159819567529e-7
        rest = rest + (coef2 * upper + (coef1 * lower + (coef3 * upper + coef2 * lower)))
        ramp = (k * offset) & (N - 1)
        ramp = jnp.where(ramp < N // 2, ramp, ramp - N).astype(F32) * (2.0 * math.pi / N)
        cosine, sine = sincos(rest + ramp)
        table[at, 0, p] = cosine * (1.0 / N)
        table[at, 1, p] = sine * (-1.0 / N)


def store_split(lhs, row, values):
    for i, (first, second) in enumerate(values):
        both = jnp.concatenate([first, second], axis=1)
        high = both.astype(BF16)
        low = (both - high.astype(F32)).astype(BF16)
        rows = slice(row + 8 * i, row + 8 * i + 8)
        lhs[rows, : 2 * LANES] = high
        lhs[rows, 2 * LANES :] = low


def product(lhs, weight):
    high, low = lhs[:, : 2 * LANES], lhs[:, 2 * LANES :]
    return jnp.dot(
        jnp.concatenate([high, low, high], axis=1), weight[...], preferred_element_type=F32
    )


def spectral_pass(field, table, twiddle, weight, left, result, batch, side=None):
    groups = batch // 8
    width = 2
    steps = 8 // width

    def row_of(values, part, p, q):
        return values[part, p, q : q + 1, :]

    def table_row(part, p, q):
        values, at = table
        return values[at, part, p, q : q + 1, :]

    def places(step):
        for j in range(width):
            for g in range(groups):
                yield step * width + j, slice(8 * g, 8 * g + 8), 64 * (groups * j + g)

    def result_rows(row, q):
        return slice(row + 8 * q, row + 8 * q + 8)

    def forward(step, lhs):
        for p, rows, row in places(step):
            x = radix8([(field[0, p, b, rows], field[1, p, b, rows]) for b in range(8)], -1)
            x = [
                c_mul(x[q], (row_of(twiddle, 0, p, q), row_of(twiddle, 1, p, q)))
                for q in range(8)
            ]
            store_split(lhs, row, x)

    def other_work(turn, i):
        if side is not None and turn is not None:
            side(2 * groups * turn + i)

    def transfer(step, values, lhs):
        for i, (p, rows, row) in enumerate(places(step)):
            other_work((0, 1, 2, None)[step], i)
            x = []
            for q in range(8):
                at = result_rows(row, q)
                value = (values[at, :LANES], values[at, LANES:])
                x.append(c_mul(value, (table_row(0, p, q), table_row(1, p, q))))
            store_split(lhs, row, [(v[1], v[0]) for v in x])

    def inverse(step, values):
        for i, (p, rows, row) in enumerate(places(step)):
            other_work((None, 3, None, None)[step], i)
            x = []
            for q in range(8):
                at = result_rows(row, q)
                value = (values[at, LANES:], values[at, :LANES])
                x.append(
                    c_mul_conj(value, (row_of(twiddle, 0, p, q), row_of(twiddle, 1, p, q)))
                )
            x = radix8(x, 1)
            for b in range(8):
                field[0, p, b, rows] = x[b][0]
                field[1, p, b, rows] = x[b][1]

    def multiply(lhs, values):
        values[...] = product(lhs, weight)

    forward_left, inverse_left = left[:2], left[2:]
    forward_result, inverse_result = result[:2], result[2:]
    forward(0, forward_left[0])
    multiply(forward_left[0], forward_result[0])
    forward(1, forward_left[1])
    multiply(forward_left[1], forward_result[1])
    transfer(0, forward_result[0], inverse_left[0])
    multiply(inverse_left[0], inverse_result[0])
    forward(2, forward_left[0])

    def two_steps(step):
        multiply(forward_left[0], forward_result[0])
        transfer(step - 1, forward_result[1], inverse_left[1])
        multiply(inverse_left[1], inverse_result[1])
        inverse(step - 2, inverse_result[0])
        forward(step + 1, forward_left[1])
        multiply(forward_left[1], forward_result[1])
        transfer(step, forward_result[0], inverse_left[0])
        multiply(inverse_left[0], inverse_result[0])
        inverse(step - 1, inverse_result[1])

    two_steps(2)
    transfer(steps - 1, forward_result[1], inverse_left[1])
    multiply(inverse_left[1], inverse_result[1])
    inverse(steps - 2, inverse_result[0])
    inverse(steps - 1, inverse_result[1])


def enter(field, b, rows, x):
    x = radix8(x, -1)
    for p in range(8):
        value = unit_root(x[p], b * p, -1)
        field[0, p, b, rows] = value[0]
        field[1, p, b, rows] = value[1]


def leave(field, b, rows):
    x = [unit_root((field[0, p, b, rows], field[1, p, b, rows]), b * p, 1) for p in range(8)]
    return radix8(x, 1)


def low_half(shape):
    return lax.broadcasted_iota(jnp.int32, shape, len(shape) - 1) < LANES // 2


def swap_halves(even, odd, low):
    crossed = pltpu.roll(jnp.where(low, odd, even), LANES // 2, 1)
    return jnp.where(low, even, crossed), jnp.where(low, crossed, odd)


def eight_rows(g):
    return pl.ds(pl.multiple_of(g * 8, 8), 8)


def pack_screen(j, scales, screen, moved, device, low):
    tiles = []
    for half in range(2):
        start = j * (2 * LANES) + half * LANES
        lanes = pl.ds(start if isinstance(j, int) else pl.multiple_of(start, LANES), LANES)
        scale = scales[0, device // 2, 2 * j + half] * (0.5 / math.pi)
        tiles.append(screen[0, :, lanes].astype(F32) * scale)
    block = jnp.concatenate(tiles, axis=0).T
    for half in range(2):
        part = block[64 * half : 64 * half + 64]
        first, second = swap_halves(part[:32], part[32:], low)
        moved[4 * j + half, 32:] = first
        moved[4 * j + 2 + half, 32:] = second


def first_rows_kernel(
    offsets_in, distances_in, scales_in, beam_in, screen_in, twiddle_in, weight_in, moved,
    field, l0, l1, l2, l3, r0, r1, r2, r3, table,
    offsets, distances, scales, beam, screen, twiddle, weight, blocks, arrival, departure,
):
    pairs = (
        (offsets_in, offsets), (distances_in, distances), (scales_in, scales),
        (twiddle_in, twiddle), (weight_in, weight), (screen_in, screen),
    )
    eights = [slice(8 * g, 8 * g + 8) for g in range(4)]
    beam_copies = [
        pltpu.make_async_copy(beam_in.at[:, rows], beam.at[:, rows], arrival.at[6 + g])
        for g, rows in enumerate(eights)
    ]
    copies = [
        pltpu.make_async_copy(source, target, arrival.at[i])
        for i, (source, target) in enumerate(pairs)
    ]
    for copy in (*copies[:2], *beam_copies, *copies[2:]):
        copy.start()
    device = lax.axis_index(AXES)
    for copy in copies[:2]:
        copy.wait()
    transfer_table(table, 0, distances[0], offsets[1])

    def leaving(part):
        at = slice(0, 128), slice(8 * part, 8 * part + 8)
        if part >= 4:
            at = slice(64 * (part - 4), 64 * (part - 4) + 64), slice(32, 64)
        return pltpu.make_async_copy(blocks.at[at], moved.at[at], departure.at[part])

    def pack(j):
        pack_screen(j, scales, screen, blocks, device, low_packed)
        if j % 16 == 15:
            leaving(4 + j // 16).start()

    low = low_half((8, LANES))

    def first(g):
        rows = slice(8 * g, 8 * g + 8)
        for b in range(8):
            x = []
            for a in range(8):
                n1 = 8 * a + b
                lanes = slice(n1 * LANES, (n1 + 1) * LANES)
                x.append((beam[0, rows, lanes], beam[1, rows, lanes]) if a < 4 else None)
            enter(field, b, rows, x)

    for g in range(4):
        beam_copies[g].wait()
        first(g)
    for copy in copies[2:]:
        copy.wait()
    low_packed = low_half((32, LANES))
    spectral_pass(
        field, (table, 0), twiddle, weight, (l0, l1, l2, l3), (r0, r1, r2, r3), 32,
        pack,
    )

    def last(g):
        rows = slice(8 * g, 8 * g + 8)
        for b in range(8):
            x = leave(field, b, rows)
            for a in range(8):
                n1 = 8 * a + b
                even, odd = swap_halves(x[a][0], x[a][1], low)
                blocks[2 * n1, rows] = even
                blocks[2 * n1 + 1, rows] = odd
        leaving(g).start()

    for g in range(4):
        last(g)
    for part in range(6):
        leaving(part).wait()


def tables_kernel(offsets, distances, scales, screen, moved, tables, phasors):
    del moved
    device = lax.axis_index(AXES)
    transfer_table(tables, 0, distances[0], offsets[0])
    transfer_table(tables, 1, distances[1], jnp.int32(0))

    def tiles(j, carry):
        for i in range(4):
            n1 = 4 * j + i
            lanes = pl.ds(pl.multiple_of(n1 * LANES, LANES), LANES)
            scale = scales[device // 4, n1] * (0.5 / math.pi)
            phasors[0, :, lanes], phasors[1, :, lanes] = phasor(
                screen[:, lanes].astype(F32) * scale
            )
        return carry

    lax.fori_loop(0, 8, tiles, 0)


def columns_kernel(
    arrived_in, tables_in, twiddle_in, weight_in, moved,
    field, l0, l1, l2, l3, r0, r1, r2, r3,
    turned, arrived, factors, tables, twiddle, weight, blocks, arrival, departure,
):
    constants = [
        pltpu.make_async_copy(source, target, arrival.at[33 + i])
        for i, (source, target) in enumerate(
            ((tables_in, tables), (twiddle_in, twiddle), (weight_in, weight))
        )
    ]

    def copy_of(n1):
        part = slice(4 * n1, 4 * n1 + 4), slice(0, 32)
        if n1 == 32:
            part = slice(0, 128), slice(32, 64)
        return pltpu.make_async_copy(arrived_in.at[part], arrived.at[part], arrival.at[n1])

    for b in range(8):
        for a in range(4):
            copy_of(8 * a + b).start()
    for copy in constants:
        copy.start()
    copy_of(32).start()

    def leaving(n1):
        rows = slice(n1 * LANES, (n1 + 1) * LANES)
        return pltpu.make_async_copy(blocks.at[rows], moved.at[rows], departure.at[n1])

    def turned_rows(slot, g):
        return turned.at[slot, 8 * g : 8 * g + 8], turned.at[slot, 8 * g + 64 : 8 * g + 72]

    for b in range(8):
        slots = [a + 4 * (b % 2) for a in range(4)]
        for a in range(4):
            copy_of(8 * a + b).wait()
        for a in range(4):
            n1 = 8 * a + b
            turned[slots[a]] = arrived[4 * n1 : 4 * n1 + 4, :32].reshape((LANES, LANES)).T
        for g in range(8):
            x = []
            for slot in slots:
                real, imag = turned_rows(slot, g)
                x.append((real[...], imag[...]))
            enter(field, b, slice(8 * g, 8 * g + 8), x + [None] * 4)

    for copy in constants:
        copy.wait()
    copy_of(32).wait()
    buffers = (l0, l1, l2, l3), (r0, r1, r2, r3)
    low = low_half((32, LANES))

    def screen_factors(n1):
        halves = swap_halves(arrived[2 * n1, 32:], arrived[2 * n1 + 1, 32:], low)
        for half in range(2):
            rows = slice(32 * half, 32 * half + 32)
            factors[0, n1, rows], factors[1, n1, rows] = phasor(halves[half])

    spectral_pass(field, (tables, 0), twiddle, weight, *buffers, 64, screen_factors)

    def middle(g, carry):
        rows = eight_rows(g)
        for b in range(8):
            x = leave(field, b, rows)
            for a in range(8):
                n1 = 8 * a + b
                x[a] = c_mul(x[a], (factors[0, n1, rows], factors[1, n1, rows]))
            enter(field, b, rows, x)
        return carry

    lax.fori_loop(0, 8, middle, 0)
    spectral_pass(field, (tables, 1), twiddle, weight, *buffers, 64)

    for b in range(8):
        slots = [a + 4 * (b % 2) for a in range(4)]
        for g in range(8):
            x = leave(field, b, slice(8 * g, 8 * g + 8))
            for a in range(4):
                real, imag = turned_rows(slots[a], g)
                real[...], imag[...] = x[a + 2]
        for a in range(4):
            n1 = 8 * a + b
            blocks[n1 * LANES : (n1 + 1) * LANES, :] = turned[slots[a]].T
            leaving(n1).start()
    for n1 in range(32):
        leaving(n1).wait()


def last_rows_kernel(
    arrived, tables, phasors, twiddle, weight, output_in_hbm,
    field, l0, l1, l2, l3, r0, r1, r2, r3, output, departure,
):
    low = low_half((8, LANES))

    def first(g):
        rows = slice(8 * g, 8 * g + 8)
        for b in range(8):
            x = []
            for a in range(8):
                n1 = 8 * a + b
                x.append(swap_halves(arrived[2 * n1, rows], arrived[2 * n1 + 1, rows], low))
            enter(field, b, rows, x)

    for g in range(4):
        first(g)
    spectral_pass(field, (tables, 1), twiddle, weight, (l0, l1, l2, l3), (r0, r1, r2, r3), 32)

    def last(g):
        rows = slice(8 * g, 8 * g + 8)
        for b in range(8):
            x = leave(field, b, rows)
            for a in range(4):
                n1 = 8 * a + b
                lanes = slice(n1 * LANES, (n1 + 1) * LANES)
                value = c_mul(x[a + 2], (phasors[0, rows, lanes], phasors[1, rows, lanes]))
                output[0, rows, lanes] = value[0]
                output[1, rows, lanes] = value[1]
        leaving(g).start()

    def leaving(g):
        rows = slice(8 * g, 8 * g + 8)
        return pltpu.make_async_copy(
            output.at[:, rows], output_in_hbm.at[:, rows], departure.at[g]
        )

    for g in range(4):
        last(g)
    for g in range(4):
        leaving(g).wait()


def call(kernel, kinds, shapes, batch, extra, flops, out_kind="v", limit=40):
    space = {"s": pltpu.SMEM, "v": pltpu.VMEM, "h": pltpu.HBM}
    scratch = [
        pltpu.VMEM((2, 8, 8, batch, LANES), F32),
        *[pltpu.VMEM((16 * batch, 4 * LANES), BF16)] * 4,
        *[pltpu.VMEM((16 * batch, 2 * LANES), F32)] * 4,
    ] if batch else []
    return pl.pallas_call(
        kernel,
        out_shape=[jax.ShapeDtypeStruct(shape, F32) for shape in shapes],
        in_specs=[pl.BlockSpec(memory_space=space[kind]) for kind in kinds],
        out_specs=[pl.BlockSpec(memory_space=space[out_kind]) for _ in shapes],
        scratch_shapes=scratch + extra,
        compiler_params=pltpu.CompilerParams(vmem_limit_bytes=limit << 20),
        cost_estimate=pl.CostEstimate(flops=flops, bytes_accessed=4 << 20, transcendentals=0),
    )


def exchange(blocks):
    return lax.all_to_all(blocks, AXES, split_axis=0, concat_axis=0, tiled=True)


def body(input_beam, offsets, distances, screens, screen_scales, last_screen, last_scales):
    twiddle, weight = (jnp.asarray(array) for array in constant_tables())
    table = (2, 8, 8, LANES)
    extra = [
        pltpu.VMEM((1, *table), F32),
        pltpu.SMEM((2,), jnp.int32),
        pltpu.SMEM((2,), F32),
        pltpu.SMEM((1, 64, 64), F32),
        pltpu.VMEM((2, 32, 4096), F32),
        pltpu.VMEM((1, 64, N), jnp.int32),
        pltpu.VMEM(twiddle.shape, F32),
        pltpu.VMEM(weight.shape, BF16),
        pltpu.VMEM((128, 64, LANES), F32),
        pltpu.SemaphoreType.DMA((10,)),
        pltpu.SemaphoreType.DMA((6,)),
    ]
    (moved,) = call(
        first_rows_kernel, "hhhhhhh", [(128, 64, LANES)], 32, extra, 10**10, "h", 60
    )(offsets, distances, screen_scales, input_beam, screens, twiddle, weight)
    tables, phasors = call(
        tables_kernel, "sssvh", [(2, *table), (2, 32, 4096)], 0, [], 10**9, "v", 60
    )(offsets, distances, last_scales, last_screen, moved)
    extra = [
        pltpu.VMEM((8, LANES, LANES), F32),
        pltpu.VMEM((128, 64, LANES), F32),
        pltpu.VMEM((2, 64, 64, LANES), F32),
        pltpu.VMEM((2, *table), F32),
        pltpu.VMEM(twiddle.shape, F32),
        pltpu.VMEM(weight.shape, BF16),
        pltpu.VMEM((4096, LANES), F32),
        pltpu.SemaphoreType.DMA((36,)),
        pltpu.SemaphoreType.DMA((32,)),
    ]
    (moved,) = call(
        columns_kernel, "hhhh", [(4096, LANES)], 64, extra, 4 * 10**10, "h", 60
    )(exchange(moved), tables, twiddle, weight)
    arrived = exchange(moved.reshape((128, 32, LANES)))
    extra = [pltpu.VMEM((2, 32, 4096), F32), pltpu.SemaphoreType.DMA((4,))]
    (output,) = call(last_rows_kernel, "vvvvv", [(2, 32, 4096)], 32, extra, 10**10, "h")(
        arrived, tables, phasors, twiddle, weight
    )
    return output


def solution(mesh):
    return jax.shard_map(
        body,
        mesh=mesh,
        in_specs=(
            P(None, AXES, None),
            P(),
            P(),
            P(None, AXES, None),
            P(),
            P(AXES, None),
            P(),
        ),
        out_specs=P(None, AXES, None),
        check_vma=False,
    )
```
